32 devices in a mesh: cplx: 4 (over y, core), dap: 8 (over z, x).
Axes of the slice: x: 2, y: 2, z: 4, core: 2. Of those that a mesh axis runs over, the one named last changes fastest.
Arguments:
- alignment_features: bfloat16 [64, 64, 256], P(('cplx', 'dap')), parts along dimension 0, may hold values from -6 to 6
- couple_features: bfloat16 [256, 64, 128], P(('cplx', 'dap')), parts along dimension 0, may hold values from -6 to 6
- alignment_presence: int32 [64, 64], P('cplx'), parts along dimension 0, may hold values 0 or 1
- amino_presence: int32 [256], P('cplx'), parts along dimension 0, may hold values 0 or 1
- strand_identity: int32 [256], P('cplx'), parts along dimension 0, may hold values from 0 to 3, never falling along the last dimension, each value on 1 to 32 neighbouring positions
- strand_couple_embedding: float32 [2, 128], replicated, may hold values from -4 to 4
- fourfold_input_matrix: bfloat16 [256, 1024], replicated, may hold values from -0.375 to 0.375
- heads_merge_matrix: bfloat16 [256, 256], replicated, may hold values from -1.5 to 1.5
- couple_logit_matrix: bfloat16 [128, 8], replicated, may hold values from -30 to 30
- twin_factor_matrix: bfloat16 [256, 64], replicated, may hold values from -0.375 to 0.375
- tensor_reduce_matrix: bfloat16 [1024, 128], replicated, may hold values from -0.75 to 0.75
Outputs:
- alignment_mixed: bfloat16 [64, 64, 256], P(('cplx', 'dap')), parts along dimension 0
- couple_refreshed: bfloat16 [256, 64, 128], P(('cplx', 'dap')), parts along dimension 0
The draws below stay inside these ranges and needn't reach their ends.
There are 4 independent parts, one for each index of `cplx`. The reference program is written for one: setup_inputs(seed, part) draws one part's arguments, and reference() takes and returns one part's arrays. A program takes and returns all parts, laid end to end along the dimension named above; an argument that names none is the same for every part. Nothing has to cross between parts.
All inputs are finite; a program needn't handle non-finite values.
Results may differ from the reference program's by a relative error of at most 0.0075.
The reference program's roundings to bfloat16 on the way count: a program that leaves them out, or rounds other values in their place, can miss the bound.
Values may be sent and summed in bfloat16 or wider, within the bound.
No kernel may reach another device: no remote copies, remote signals or barrier semaphores. Data moves between devices by JAX's collectives and lax.ppermute only.
A program may use at most 64 MiB of HBM per device.

```python
import math
import jax
import jax.numpy as jnp
import numpy as np
from jax import lax

FEATURE_DEPTH = 256
CZ = 128
HEAD_NUMBER = 8
HEAD_DEPTH = 32
TENSOR_WIDTH = 32
ALIGNED_SEQS = 16
AMINO_COUNT = 64


def draw_couple_logit_matrix(key, part):
    first, second = jax.random.split(jax.random.fold_in(key, 11))
    base = jax.random.truncated_normal(first, -3.0, 3.0, (CZ, HEAD_NUMBER), jnp.float32)
    spread = 0.15 + 0.0 * jax.random.uniform(second, (1, HEAD_NUMBER), jnp.float32)
    return (base * spread).astype(jnp.bfloat16)


def place_ends(drawn, stream_key, smallest, high):
    spot = [jax.random.randint(jax.random.fold_in(stream_key, axis), (), 0, length) for axis, length in enumerate(drawn.shape)]
    longest = drawn.shape.index(max(drawn.shape))
    neighbour = spot[:longest] + [(spot[longest] + 1) % drawn.shape[longest]] + spot[longest + 1:]
    return drawn.at[tuple(spot)].set(smallest).at[tuple(neighbour)].set(high)


def levels(stream_key, extent, cuts, smallest, top_value):
    factor_of = 1.0
    for dim, blocks in cuts:
        steps = jax.random.uniform(jax.random.fold_in(jax.random.fold_in(stream_key, 6), dim), (blocks,), jnp.float32, smallest / len(cuts), top_value / len(cuts))
        factor_of = factor_of * jnp.repeat(jnp.exp(steps), extent[dim] // blocks).reshape((-1,) + (1,) * (len(extent) - 1 - dim))
    return factor_of


def split_up(count, total, reach, slope):
    weights = [(1 << 20) // math.isqrt(standing ** slope) + 1 for standing in range(2, count + 1)]
    rest, given = total - reach - (count - 1), [1] * (count - 1)
    while rest > 0:
        candidates = [i for i in range(count - 1) if given[i] < reach]
        pool, left = sum([weights[i] for i in candidates]), rest
        for i in candidates:
            addition = min(reach - given[i], max(1, left * weights[i] // pool), rest)
            given[i] = given[i] + addition
            rest = rest - addition
    return np.array([reach] + given)


def uneven(own_key, number_of, total, reach, skew):
    if number_of == 2:
        one = jax.random.randint(own_key, (), max(1, total - reach), min(reach, total - 1) + 1)
        return jnp.stack([one, total - one])
    tallies = jnp.asarray(split_up(number_of, total, reach, skew), jnp.int32)
    pairs = (number_of - 1) // 2
    donor, sink = tallies[1:1 + 2 * pairs:2], tallies[2:2 + 2 * pairs:2]
    margin = jnp.minimum(donor - 1, reach - sink)
    passed = jax.random.randint(jax.random.fold_in(own_key, 1), (pairs,), 0, 1 << 20) % (margin + 1)
    tallies = tallies.at[1:1 + 2 * pairs:2].set(donor - passed).at[2:2 + 2 * pairs:2].set(sink + passed)
    return tallies[jax.random.permutation(jax.random.fold_in(own_key, 2), number_of)]


def normal_values(own_key, shape, width, limit, pieces=(), held_as=jnp.bfloat16):
    result = jax.random.normal(own_key, shape, jnp.float32) * width
    if len(pieces) > 0:
        result = levels(own_key, shape, pieces, -0.22, 0.18) * result
    return jnp.clip(result, min=-limit, max=limit).astype(held_as)


def setup_inputs(seed: int = 0, part: int = 0) -> dict:
    keys = jax.random.split(jax.random.key(seed), 12)
    part_keys = jax.random.split(jax.random.fold_in(keys[11], part), 12)
    alignment_features = normal_values(part_keys[0], (ALIGNED_SEQS, AMINO_COUNT, FEATURE_DEPTH), 1.0, 6.0, ((0, 8),))
    couple_features = normal_values(part_keys[1], (AMINO_COUNT, AMINO_COUNT, CZ), 1.0, 6.0, ((0, 8),))
    alignment_presence = place_ends((jax.random.randint(part_keys[2], (ALIGNED_SEQS, AMINO_COUNT), 0, 4) < 3).astype(jnp.int32), jax.random.fold_in(part_keys[2], 1), 0, 1)
    amino_presence = place_ends((jax.random.randint(part_keys[3], (AMINO_COUNT,), 0, 8) < 7).astype(jnp.int32), jax.random.fold_in(part_keys[3], 1), 0, 1)
    strand_identity = jnp.searchsorted(jnp.cumsum(uneven(part_keys[4], 4, AMINO_COUNT, AMINO_COUNT // 2, 0)), jnp.arange(AMINO_COUNT), side="right").astype(jnp.int32)
    strand_couple_embedding = normal_values(keys[5], (2, CZ), 1.0, 4.0, (), jnp.float32)
    fourfold_input_matrix = normal_values(keys[6], (FEATURE_DEPTH, 4 * HEAD_NUMBER * HEAD_DEPTH), FEATURE_DEPTH ** -0.5, 0.375)
    heads_merge_matrix = normal_values(keys[7], (HEAD_NUMBER * HEAD_DEPTH, FEATURE_DEPTH), (HEAD_NUMBER * HEAD_DEPTH // 16) ** -0.5, 1.5)
    couple_logit_matrix = draw_couple_logit_matrix(jax.random.fold_in(keys[11], 71), part)
    twin_factor_matrix = normal_values(keys[9], (FEATURE_DEPTH, 2 * TENSOR_WIDTH), FEATURE_DEPTH ** -0.5, 0.375)
    tensor_reduce_matrix = normal_values(keys[10], (TENSOR_WIDTH * TENSOR_WIDTH, CZ), (TENSOR_WIDTH * 2) ** -0.5, 0.75)
    return dict(alignment_features=alignment_features, couple_features=couple_features, alignment_presence=alignment_presence, amino_presence=amino_presence, strand_identity=strand_identity, strand_couple_embedding=strand_couple_embedding, fourfold_input_matrix=fourfold_input_matrix, heads_merge_matrix=heads_merge_matrix, couple_logit_matrix=couple_logit_matrix, twin_factor_matrix=twin_factor_matrix, tensor_reduce_matrix=tensor_reduce_matrix)


EPS = 1e-05

def standardize_features(x):
    x = x.astype(jnp.float32)
    center = x - lax.optimization_barrier(jnp.mean(x, axis=-1, keepdims=True))
    spread = lax.optimization_barrier(jnp.mean(center * center, axis=-1, keepdims=True))
    return center * lax.rsqrt(spread + EPS)

def reference(alignment_features, couple_features, alignment_presence, amino_presence, strand_identity, strand_couple_embedding, fourfold_input_matrix, heads_merge_matrix, couple_logit_matrix, twin_factor_matrix, tensor_reduce_matrix):
    same = (strand_identity[:, None] == strand_identity[None, :]).astype(jnp.float32)[..., None]
    z_in = couple_features.astype(jnp.float32) + (1.0 - same) * strand_couple_embedding[0] + same * strand_couple_embedding[1]
    pair_ln = standardize_features(z_in).astype(jnp.bfloat16)
    bias = jnp.einsum('ijc,ch->hij', pair_ln.astype(jnp.float32), couple_logit_matrix.astype(jnp.float32)).astype(jnp.bfloat16)
    standardized_alignment = standardize_features(alignment_features).astype(jnp.bfloat16)
    mapped_lines = jnp.dot(standardized_alignment.reshape(ALIGNED_SEQS * AMINO_COUNT, FEATURE_DEPTH), fourfold_input_matrix, preferred_element_type=jnp.float32)
    mapped_lines = mapped_lines.reshape(ALIGNED_SEQS, AMINO_COUNT, 4, HEAD_NUMBER, HEAD_DEPTH)
    asking_vectors = (mapped_lines[:, :, 0] * HEAD_DEPTH ** (-0.5)).astype(jnp.bfloat16)
    target_vectors = mapped_lines[:, :, 1].astype(jnp.bfloat16)
    content_vectors = mapped_lines[:, :, 2].astype(jnp.bfloat16)
    sigmoid_factors = jax.nn.sigmoid(mapped_lines[:, :, 3])
    presence_numeric = alignment_presence.astype(jnp.float32)
    absent_target_penalty = (presence_numeric - 1.0) * 1000000000.0

    def lone_aligned_line(element_list):
        qrow, krow, vrow, grow, kbias, mrow = element_list
        scores = jnp.einsum('ihd,jhd->hij', qrow.astype(jnp.float32), krow.astype(jnp.float32))
        scores = scores + bias.astype(jnp.float32) + kbias[None, None, :]
        weights = jax.nn.softmax(scores, axis=-1).astype(jnp.bfloat16)
        context = jnp.einsum('hij,jhd->ihd', weights.astype(jnp.float32), vrow.astype(jnp.float32))
        gated_values = (grow * context).astype(jnp.bfloat16).reshape(AMINO_COUNT, HEAD_NUMBER * HEAD_DEPTH)
        offset_lines = jnp.dot(gated_values, heads_merge_matrix, preferred_element_type=jnp.float32)
        return (mrow.astype(jnp.float32) + offset_lines).astype(jnp.bfloat16)
    alignment_mixed = lax.map(lone_aligned_line, (asking_vectors, target_vectors, content_vectors, sigmoid_factors, absent_target_penalty, alignment_features))
    twin_factor_features = jnp.dot(standardize_features(alignment_mixed).astype(jnp.bfloat16).reshape(ALIGNED_SEQS * AMINO_COUNT, FEATURE_DEPTH), twin_factor_matrix, preferred_element_type=jnp.float32)
    twin_factor_features = twin_factor_features.reshape(ALIGNED_SEQS, AMINO_COUNT, 2 * TENSOR_WIDTH)
    left = (twin_factor_features[:, :, :TENSOR_WIDTH] * presence_numeric[..., None]).astype(jnp.bfloat16)
    right = (twin_factor_features[:, :, TENSOR_WIDTH:] * presence_numeric[..., None]).astype(jnp.bfloat16)
    count = jnp.dot(presence_numeric.T, presence_numeric, precision=lax.Precision.HIGHEST) + 1.0

    def one_residue(element_list):
        left_i, count_i = element_list
        outer = jnp.einsum('sc,sje->jce', left_i.astype(jnp.float32), right.astype(jnp.float32))
        outer = outer.astype(jnp.bfloat16).reshape(AMINO_COUNT, TENSOR_WIDTH * TENSOR_WIDTH)
        return jnp.dot(outer, tensor_reduce_matrix, preferred_element_type=jnp.float32) / count_i[:, None]
    update = lax.map(one_residue, (jnp.transpose(left, (1, 0, 2)), count))
    resf = amino_presence.astype(jnp.float32)
    pair_mask = resf[:, None] * resf[None, :]
    couple_refreshed = (z_in + pair_mask[..., None] * update).astype(jnp.bfloat16)
    return (alignment_mixed, couple_refreshed)
```

```python
import functools

import jax
import jax.numpy as jnp
from jax import lax
from jax.experimental import pallas as pl
from jax.experimental.pallas import tpu as pltpu
from jax.sharding import PartitionSpec as P

EPS = 1e-05
LANES = 128
F32 = jnp.float32
BF16 = jnp.bfloat16
VMEM_LIMIT = 24 * 1024 * 1024


def standardize(x):
    center = x - jnp.mean(x, axis=-1, keepdims=True)
    spread = jnp.mean(center * center, axis=-1, keepdims=True)
    return center * lax.rsqrt(spread + EPS)


def to_column(row, size):
    down = lax.broadcasted_iota(jnp.int32, (size, size), 0)
    across = lax.broadcasted_iota(jnp.int32, (size, size), 1)
    spread = jnp.where(down == across, jnp.broadcast_to(row, (size, size)), 0.0)
    return jnp.sum(spread, axis=1, keepdims=True)


def dot(a, b, contract):
    return lax.dot_general(a, b, (contract, ((), ())), preferred_element_type=F32)


NN = ((1,), (0,))
NT = ((1,), (1,))
TN = ((0,), (0,))


def pair_input(ids, ids_row, emb, x, res_start):
    rows, size, channels = x.shape
    chain = jnp.broadcast_to(to_column(ids_row[...].astype(F32), size), (size, channels))
    other, same = emb[0:1, :], emb[1:2, :]
    for i in range(rows):
        chain_i = ids[res_start + i].astype(F32)
        yield x[i].astype(F32) + jnp.where(chain == chain_i, same, other)


def bias_kernel(ids, ids_row, emb, x, logit, out):
    rows, size, _ = x.shape
    heads = logit.shape[0]
    group = heads * rows
    pack = LANES // group
    part = size // pack
    res_start = lax.axis_index("dap") * rows
    head = lax.broadcasted_iota(jnp.int32, (heads, LANES), 0)
    lane = lax.broadcasted_iota(jnp.int32, (heads, LANES), 1)
    spread = jnp.where((lane % group) // rows == head, 1.0, 0.0).astype(BF16)
    wide = dot(logit[...], spread, TN).astype(BF16)
    normed = [standardize(z).astype(BF16) for z in pair_input(ids, ids_row, emb, x, res_start)]
    full = dot(jnp.concatenate(normed, axis=0), wide, NN)
    lane = lax.broadcasted_iota(jnp.int32, (part, LANES), 1)
    total = jnp.zeros((part, LANES), F32)
    for i in range(rows):
        for half in range(pack):
            begin = i * size + half * part
            pick = (lane // group == half) & (lane % rows == i)
            total = jnp.where(pick, full[begin : begin + part, :], total)
    total = total.astype(BF16)
    for peer in range(out.shape[0]):
        out[peer] = total


def project_kernel(rows, x, weights, presence, scores, content, gate, present, present_row):
    seqs, size, depth = x.shape
    merged = content.shape[2]
    group_total = scores.shape[2]
    heads = group_total // size
    head_size = merged // heads
    seq_start = lax.axis_index("dap") * seqs
    normed = standardize(x[...].reshape(seqs * size, depth).astype(F32)).astype(BF16)
    mapped = dot(normed, weights[...], NN)
    asking = (mapped[:, :merged] * head_size**-0.5).astype(BF16).astype(F32)
    target = mapped[:, merged : 2 * merged].astype(BF16)
    content[...] = mapped[:, 2 * merged : 3 * merged].astype(BF16).reshape(content.shape)
    gate[...] = jax.nn.sigmoid(mapped[:, 3 * merged :]).reshape(gate.shape)
    lane = lax.broadcasted_iota(jnp.int32, (rows, merged), 1)
    row_pieces = []
    for s in range(seqs):
        pieces = []
        for begin in range(s * size, (s + 1) * size, rows):
            here = asking[begin : begin + rows, :]
            for h in range(heads):
                pieces.append(jnp.where(lane // head_size == h, here, 0.0))
        spread = jnp.concatenate(pieces, axis=0).astype(BF16)
        scores[s] = dot(target[s * size : (s + 1) * size, :], spread, NT)
        row = presence[pl.ds(seq_start + s, 1), :].astype(F32)
        present[s] = jnp.broadcast_to(to_column(row, size), (size, LANES))
        row_pieces.append(row)
    present_row[...] = jnp.concatenate(row_pieces, axis=1)


def attend_kernel(bias, scores, content, gate, present, present_row, x, merge, twin, mixed, out):
    devices, part, _ = bias.shape
    seqs, size, depth = x.shape
    merged = content.shape[2]
    pack = size // part
    group = LANES // pack
    rows = size // devices
    heads = group // rows
    head_size = merged // heads
    width = twin.shape[0] // 2
    lane = lax.broadcasted_iota(jnp.int32, (rows, merged), 1)
    gated = []
    tables = []
    for block in range(devices // pack):
        got = [bias[block * pack + n].astype(F32) for n in range(pack)]
        tables.append(
            jnp.concatenate(
                [
                    jnp.concatenate([g[:, half * group : (half + 1) * group] for g in got], axis=1)
                    for half in range(pack)
                ],
                axis=0,
            )
        )
    for s in range(seqs):
        absent = (present[s] - 1.0) * 1000000000.0
        context = []
        for block in range(devices // pack):
            logits = scores[s, :, block * LANES : (block + 1) * LANES] + tables[block] + absent
            raised = jnp.exp(logits - jnp.max(logits, axis=0, keepdims=True))
            weights = raised * (1.0 / jnp.sum(raised, axis=0, keepdims=True))
            mixed_heads = dot(weights.astype(BF16), content[s], TN)
            for n in range(pack):
                total = jnp.zeros((rows, merged), F32)
                for h in range(heads):
                    begin = n * group + h * rows
                    total = jnp.where(lane // head_size == h, mixed_heads[begin : begin + rows, :], total)
                context.append(total)
        gated.append((gate[s] * jnp.concatenate(context, axis=0)).astype(BF16))
    offset = dot(jnp.concatenate(gated, axis=0), merge[...], NN)
    updated = (x[...].reshape(seqs * size, depth).astype(F32) + offset).astype(BF16)
    mixed[...] = updated.reshape(mixed.shape)
    normed = standardize(updated.astype(F32)).astype(BF16)
    left = dot(normed, twin[...], NT)
    right = (dot(twin[width:, :], normed, NT) * present_row[...]).astype(BF16)
    blocks = seqs * size // LANES
    for peer in range(devices):
        for block in range(blocks):
            out[peer, block * width : (block + 1) * width, :] = right[:, block * LANES : (block + 1) * LANES]
    for peer in range(devices):
        rows_here = []
        for s in range(seqs):
            begin = peer * rows
            here = left[s * size + begin : s * size + begin + rows, :]
            rows_here.append(here * present[s, begin : begin + rows, : 2 * width])
        piece = jnp.concatenate(rows_here, axis=0)
        piece = jnp.concatenate([piece, jnp.zeros((seqs * rows, LANES - 2 * width), F32)], axis=1)
        out[peer, blocks * width :, :] = piece.astype(BF16)


def prepare_kernel(ids, amino, ids_row, amino_row, emb, x, presence, reduce, pair, scale, spread, wide):
    rows, size, channels = x.shape
    width = spread.shape[0]
    res_start = lax.axis_index("dap") * rows
    for i, z in enumerate(pair_input(ids, ids_row, emb, x, res_start)):
        pair[i] = z
    here = presence[...].astype(BF16)
    count = dot(here, here, TN)
    lane = lax.broadcasted_iota(jnp.int32, (size, size), 1)
    kept = to_column(amino_row[...].astype(F32), size)
    for i in range(rows):
        column = jnp.sum(jnp.where(lane == res_start + i, count, 0.0), axis=1, keepdims=True) + 1.0
        kept_i = amino[res_start + i].astype(F32)
        scale[i] = jnp.broadcast_to(kept * kept_i / column, (size, channels))
    wide[...] = reduce[...].astype(F32)
    for e in range(width):
        spread[:, e * channels : (e + 1) * channels] = wide[pl.ds(e, width, stride=width), :].astype(BF16)


def outer_kernel(got, spread, pair, scale, out, right_rows, left_rows):
    devices = got.shape[0]
    rows, size, channels = pair.shape
    width = spread.shape[0]
    blocks = right_rows.shape[0]
    seqs = blocks * LANES // size
    for peer in range(devices):
        for block in range(blocks):
            right_rows[block, pl.ds(peer, width, stride=devices), :] = got[
                peer, block * width : (block + 1) * width, :
            ].astype(F32)
        left_rows[pl.ds(peer, seqs * rows, stride=devices), :] = got[peer, blocks * width :, :].astype(F32)
    right = jnp.concatenate([jnp.transpose(right_rows[block]) for block in range(blocks)], axis=0).astype(BF16)
    left = left_rows[...][:, :width].astype(BF16)
    table = dot(left, spread[...], NN)
    for i in range(rows):
        update = jnp.zeros((size, channels), F32)
        for s in range(seqs):
            begin = (s * rows + i) * devices
            columns = jnp.concatenate(
                [table[begin : begin + devices, e * channels : (e + 1) * channels] for e in range(width)], axis=0
            ).astype(BF16)
            update = update + dot(right[s * size : (s + 1) * size, :], columns, NN)
        out[i] = (pair[i] + scale[i] * update).astype(BF16)


def vmem(count):
    return [pl.BlockSpec(memory_space=pltpu.VMEM) for _ in range(count)]


def smem(count):
    return [pl.BlockSpec(memory_space=pltpu.SMEM) for _ in range(count)]


def call(body, shapes, in_specs, name, flops, moved, scratch=()):
    return pl.pallas_call(
        body,
        out_shape=shapes,
        in_specs=in_specs,
        out_specs=jax.tree.map(lambda _: pl.BlockSpec(memory_space=pltpu.VMEM), shapes),
        scratch_shapes=list(scratch),
        compiler_params=pltpu.CompilerParams(vmem_limit_bytes=VMEM_LIMIT),
        cost_estimate=pl.CostEstimate(flops=flops, bytes_accessed=moved, transcendentals=0),
        name=name,
    )


def on_device(
    alignment_features,
    couple_features,
    alignment_presence,
    amino_presence,
    strand_identity,
    strand_couple_embedding,
    fourfold_input_matrix,
    heads_merge_matrix,
    couple_logit_matrix,
    twin_factor_matrix,
    tensor_reduce_matrix,
):
    rows, size, channels = couple_features.shape
    seqs, _, depth = alignment_features.shape
    devices = size // rows
    heads = couple_logit_matrix.shape[1]
    merged = heads_merge_matrix.shape[0]
    width = twin_factor_matrix.shape[1] // 2
    group = heads * rows
    pack = LANES // group
    struct = jax.ShapeDtypeStruct
    ids_row = strand_identity.reshape(1, size)
    amino_row = amino_presence.reshape(1, size)

    bias = call(
        bias_kernel,
        struct((devices, size // pack, LANES), BF16),
        smem(1) + vmem(4),
        "pair_bias",
        2 * rows * size * channels * LANES,
        2 * rows * size * channels,
    )(strand_identity, ids_row, strand_couple_embedding, couple_features, couple_logit_matrix.T)
    bias = lax.all_to_all(bias, "dap", 0, 0)

    scores, content, gate, present, present_row = call(
        functools.partial(project_kernel, rows),
        (
            struct((seqs, size, heads * size), F32),
            struct((seqs, size, merged), BF16),
            struct((seqs, size, merged), F32),
            struct((seqs, size, LANES), F32),
            struct((1, seqs * size), F32),
        ),
        vmem(3),
        "project",
        2 * seqs * size * depth * 4 * merged + 2 * seqs * size * size * heads * merged,
        2 * depth * 4 * merged,
    )(alignment_features, fourfold_input_matrix, alignment_presence)

    blocks = seqs * size // LANES
    mixed, factors = call(
        attend_kernel,
        (
            struct(alignment_features.shape, BF16),
            struct((devices, blocks * width + seqs * rows, LANES), BF16),
        ),
        vmem(9),
        "attend",
        4 * seqs * size * size * heads * merged,
        8 * seqs * size * size * heads,
    )(
        bias,
        scores,
        content,
        gate,
        present,
        present_row,
        alignment_features,
        heads_merge_matrix,
        twin_factor_matrix.T,
    )
    factors = lax.all_to_all(factors, "dap", 0, 0)

    pair, scale, spread = call(
        prepare_kernel,
        (
            struct(couple_features.shape, F32),
            struct(couple_features.shape, F32),
            struct((width, width * channels), BF16),
        ),
        smem(2) + vmem(6),
        "prepare",
        16 * rows * size * channels,
        16 * rows * size * channels,
        [pltpu.VMEM((width * width, channels), F32)],
    )(
        strand_identity,
        amino_presence,
        ids_row,
        amino_row,
        strand_couple_embedding,
        couple_features,
        alignment_presence,
        tensor_reduce_matrix,
    )

    refreshed = call(
        outer_kernel,
        struct(couple_features.shape, BF16),
        vmem(4),
        "outer_mean",
        4 * rows * size * channels * width * seqs * devices,
        16 * rows * size * channels,
        [
            pltpu.VMEM((blocks, width * devices, LANES), F32),
            pltpu.VMEM((seqs * rows * devices, LANES), F32),
        ],
    )(factors, spread, pair, scale)
    return (mixed, refreshed)


def solution(mesh):
    in_specs = (
        P(("cplx", "dap"), None, None),
        P(("cplx", "dap"), None, None),
        P("cplx", None),
        P("cplx"),
        P("cplx"),
        P(),
        P(),
        P(),
        P(),
        P(),
        P(),
    )
    out_specs = (P(("cplx", "dap"), None, None), P(("cplx", "dap"), None, None))
    return jax.shard_map(
        on_device, mesh=mesh, in_specs=in_specs, out_specs=out_specs, check_vma=False
    )
```

```python
import functools

import jax
import jax.numpy as jnp
from jax import lax
from jax.experimental import pallas as pl
from jax.experimental.pallas import tpu as pltpu
from jax.sharding import PartitionSpec as P

EPS = 1e-05
LANES = 128
F32 = jnp.float32
BF16 = jnp.bfloat16
VMEM_LIMIT = 24 * 1024 * 1024
VMEM_FULL = 63 * 1024 * 1024


def standardize(x):
    center = x - jnp.mean(x, axis=-1, keepdims=True)
    spread = jnp.mean(center * center, axis=-1, keepdims=True)
    return center * lax.rsqrt(spread + EPS)


def to_column(row, size):
    down = lax.broadcasted_iota(jnp.int32, (size, size), 0)
    across = lax.broadcasted_iota(jnp.int32, (size, size), 1)
    spread = jnp.where(down == across, jnp.broadcast_to(row, (size, size)), 0.0)
    return jnp.sum(spread, axis=1, keepdims=True)


def dot(a, b, contract):
    return lax.dot_general(a, b, (contract, ((), ())), preferred_element_type=F32)


NN = ((1,), (0,))
NT = ((1,), (1,))
TN = ((0,), (0,))


def pair_input(ids_row, emb, x, chains, res_start):
    rows, size, channels = x.shape
    chain = jnp.broadcast_to(to_column(ids_row[...].astype(F32), size), (size, channels))
    chains[...] = chain
    other, same = emb[0:1, :], emb[1:2, :]
    for i in range(rows):
        chain_i = chains[pl.ds(res_start + i, 1), :]
        yield x[i].astype(F32) + jnp.where(chain == chain_i, same, other)


def bias_kernel(ids_row, emb, x, logit, out, chains):
    rows, size, _ = x.shape
    heads = logit.shape[0]
    group = heads * rows
    pack = LANES // group
    part = size // pack
    res_start = lax.axis_index("dap") * rows
    head = lax.broadcasted_iota(jnp.int32, (heads, LANES), 0)
    lane = lax.broadcasted_iota(jnp.int32, (heads, LANES), 1)
    spread = jnp.where((lane % group) // rows == head, 1.0, 0.0).astype(BF16)
    wide = dot(logit[...], spread, TN).astype(BF16)
    normed = [standardize(z).astype(BF16) for z in pair_input(ids_row, emb, x, chains, res_start)]
    full = dot(jnp.concatenate(normed, axis=0), wide, NN)
    lane = lax.broadcasted_iota(jnp.int32, (part, LANES), 1)
    total = jnp.zeros((part, LANES), F32)
    for i in range(rows):
        for half in range(pack):
            begin = i * size + half * part
            pick = (lane // group == half) & (lane % rows == i)
            total = jnp.where(pick, full[begin : begin + part, :], total)
    total = total.astype(BF16)
    for peer in range(out.shape[0]):
        out[peer] = total


def project_kernel(rows, x, weights, presence, scores, content, gate, present, present_row):
    seqs, size, depth = x.shape
    merged = content.shape[2]
    group_total = scores.shape[2]
    heads = group_total // size
    head_size = merged // heads
    seq_start = lax.axis_index("dap") * seqs
    normed = standardize(x[...].reshape(seqs * size, depth).astype(F32)).astype(BF16)
    mapped = dot(normed, weights[...], NN)
    asking = (mapped[:, :merged] * head_size**-0.5).astype(BF16).astype(F32)
    target = mapped[:, merged : 2 * merged].astype(BF16)
    content[...] = mapped[:, 2 * merged : 3 * merged].astype(BF16).reshape(content.shape)
    gate[...] = jax.nn.sigmoid(mapped[:, 3 * merged :]).reshape(gate.shape)
    lane = lax.broadcasted_iota(jnp.int32, (rows, merged), 1)
    row_pieces = []
    for s in range(seqs):
        pieces = []
        for begin in range(s * size, (s + 1) * size, rows):
            here = asking[begin : begin + rows, :]
            for h in range(heads):
                pieces.append(jnp.where(lane // head_size == h, here, 0.0))
        spread = jnp.concatenate(pieces, axis=0).astype(BF16)
        scores[s] = dot(target[s * size : (s + 1) * size, :], spread, NT)
        row = presence[pl.ds(seq_start + s, 1), :].astype(F32)
        present[s] = jnp.broadcast_to(to_column(row, size), (size, LANES))
        row_pieces.append(row)
    present_row[...] = jnp.concatenate(row_pieces, axis=1)


def attend_kernel(order, bias, scores, content, gate, present, present_row, x, merge, twin, mixed, out):
    devices, part, _ = bias.shape
    seqs, size, depth = x.shape
    merged = content.shape[2]
    pack = size // part
    group = LANES // pack
    rows = size // devices
    heads = group // rows
    head_size = merged // heads
    width = twin.shape[0] // 2
    lane = lax.broadcasted_iota(jnp.int32, (rows, merged), 1)
    gated = []
    tables = []
    for block in range(devices // pack):
        got = [bias[order.index(block * pack + n)].astype(F32) for n in range(pack)]
        tables.append(
            jnp.concatenate(
                [
                    jnp.concatenate([g[:, half * group : (half + 1) * group] for g in got], axis=1)
                    for half in range(pack)
                ],
                axis=0,
            )
        )
    for s in range(seqs):
        absent = (present[s] - 1.0) * 1000000000.0
        context = []
        for block in range(devices // pack):
            logits = scores[s, :, block * LANES : (block + 1) * LANES] + tables[block] + absent
            raised = jnp.exp(logits - jnp.max(logits, axis=0, keepdims=True))
            weights = raised * (1.0 / jnp.sum(raised, axis=0, keepdims=True))
            mixed_heads = dot(weights.astype(BF16), content[s], TN)
            for n in range(pack):
                total = jnp.zeros((rows, merged), F32)
                for h in range(heads):
                    begin = n * group + h * rows
                    total = jnp.where(lane // head_size == h, mixed_heads[begin : begin + rows, :], total)
                context.append(total)
        gated.append((gate[s] * jnp.concatenate(context, axis=0)).astype(BF16))
    offset = dot(jnp.concatenate(gated, axis=0), merge[...], NN)
    updated = (x[...].reshape(seqs * size, depth).astype(F32) + offset).astype(BF16)
    mixed[...] = updated.reshape(mixed.shape)
    normed = standardize(updated.astype(F32)).astype(BF16)
    left = dot(normed, twin[...], NT)
    right = (dot(twin[width:, :], normed, NT) * present_row[...]).astype(BF16)
    blocks = seqs * size // LANES
    for peer in range(devices):
        for block in range(blocks):
            out[peer, block * width : (block + 1) * width, :] = right[:, block * LANES : (block + 1) * LANES]
    for slot, peer in enumerate(order):
        rows_here = []
        for s in range(seqs):
            begin = peer * rows
            here = left[s * size + begin : s * size + begin + rows, :]
            rows_here.append(here * present[s, begin : begin + rows, : 2 * width])
        piece = jnp.concatenate(rows_here, axis=0)
        piece = jnp.concatenate([piece, jnp.zeros((seqs * rows, LANES - 2 * width), F32)], axis=1)
        out[slot, blocks * width :, :] = piece.astype(BF16)


def prepare_kernel(ids_row, amino_row, emb, x, presence, reduce, pair, scale, spread, wide, chains, keeps):
    rows, size, channels = x.shape
    width = spread.shape[0]
    res_start = lax.axis_index("dap") * rows
    for i, z in enumerate(pair_input(ids_row, emb, x, chains, res_start)):
        pair[i] = z
    here = presence[...].astype(BF16)
    count = dot(here, here, TN)
    lane = lax.broadcasted_iota(jnp.int32, (size, size), 1)
    kept = jnp.broadcast_to(to_column(amino_row[...].astype(F32), size), (size, channels))
    keeps[...] = kept
    for i in range(rows):
        column = jnp.sum(jnp.where(lane == res_start + i, count, 0.0), axis=1, keepdims=True) + 1.0
        scale[i] = kept * keeps[pl.ds(res_start + i, 1), :] / column
    wide[...] = reduce[...].astype(F32)
    for e in range(width):
        spread[:, e * channels : (e + 1) * channels] = wide[pl.ds(e, width, stride=width), :].astype(BF16)


def outer_kernel(order, got, spread, pair, scale, out, right_rows, left_rows):
    devices = got.shape[0]
    rows, size, channels = pair.shape
    width = spread.shape[0]
    blocks = right_rows.shape[0]
    seqs = blocks * LANES // size
    for slot, peer in enumerate(order):
        for block in range(blocks):
            right_rows[block, pl.ds(peer, width, stride=devices), :] = got[
                slot, block * width : (block + 1) * width, :
            ].astype(F32)
        left_rows[pl.ds(peer, seqs * rows, stride=devices), :] = got[slot, blocks * width :, :].astype(F32)
    right = jnp.concatenate([jnp.transpose(right_rows[block]) for block in range(blocks)], axis=0).astype(BF16)
    left = left_rows[...][:, :width].astype(BF16)
    table = dot(left, spread[...], NN)
    for i in range(rows):
        update = jnp.zeros((size, channels), F32)
        for s in range(seqs):
            begin = (s * rows + i) * devices
            columns = jnp.concatenate(
                [table[begin : begin + devices, e * channels : (e + 1) * channels] for e in range(width)], axis=0
            ).astype(BF16)
            update = update + dot(right[s * size : (s + 1) * size, :], columns, NN)
        out[i] = (pair[i] + scale[i] * update).astype(BF16)


def member_order(devices):
    return [(5 * devices // 8 - n) % devices for n in range(devices)]


def vmem(count):
    return [pl.BlockSpec(memory_space=pltpu.VMEM) for _ in range(count)]


def call(body, shapes, in_specs, name, flops, moved, scratch=(), limit=VMEM_LIMIT):
    return pl.pallas_call(
        body,
        out_shape=shapes,
        in_specs=in_specs,
        out_specs=jax.tree.map(lambda _: pl.BlockSpec(memory_space=pltpu.VMEM), shapes),
        scratch_shapes=list(scratch),
        compiler_params=pltpu.CompilerParams(vmem_limit_bytes=limit),
        cost_estimate=pl.CostEstimate(flops=flops, bytes_accessed=moved, transcendentals=0),
        name=name,
    )


def on_device(
    alignment_features,
    couple_features,
    alignment_presence,
    amino_presence,
    strand_identity,
    strand_couple_embedding,
    fourfold_input_matrix,
    heads_merge_matrix,
    couple_logit_matrix,
    twin_factor_matrix,
    tensor_reduce_matrix,
):
    rows, size, channels = couple_features.shape
    seqs, _, depth = alignment_features.shape
    devices = size // rows
    heads = couple_logit_matrix.shape[1]
    merged = heads_merge_matrix.shape[0]
    width = twin_factor_matrix.shape[1] // 2
    group = heads * rows
    pack = LANES // group
    struct = jax.ShapeDtypeStruct
    order = member_order(devices)
    ids_row = strand_identity.reshape(1, size)
    amino_row = amino_presence.reshape(1, size)

    bias = call(
        bias_kernel,
        struct((devices, size // pack, LANES), BF16),
        vmem(4),
        "pair_bias",
        2 * rows * size * channels * LANES,
        2 * rows * size * channels,
        [pltpu.VMEM((size, channels), F32)],
        VMEM_FULL,
    )(ids_row, strand_couple_embedding, couple_features, couple_logit_matrix.T)
    bias = lax.all_to_all(bias, "dap", 0, 0, axis_index_groups=[order])

    scores, content, gate, present, present_row = call(
        functools.partial(project_kernel, rows),
        (
            struct((seqs, size, heads * size), F32),
            struct((seqs, size, merged), BF16),
            struct((seqs, size, merged), F32),
            struct((seqs, size, LANES), F32),
            struct((1, seqs * size), F32),
        ),
        vmem(3),
        "project",
        2 * seqs * size * depth * 4 * merged + 2 * seqs * size * size * heads * merged,
        2 * depth * 4 * merged,
    )(alignment_features, fourfold_input_matrix, alignment_presence)

    blocks = seqs * size // LANES
    mixed, factors = call(
        functools.partial(attend_kernel, order),
        (
            pltpu.VMEM(alignment_features.shape, BF16),
            struct((devices, blocks * width + seqs * rows, LANES), BF16),
        ),
        vmem(9),
        "attend",
        4 * seqs * size * size * heads * merged,
        8 * seqs * size * size * heads,
    )(
        bias,
        scores,
        content,
        gate,
        present,
        present_row,
        alignment_features,
        heads_merge_matrix,
        twin_factor_matrix.T,
    )
    factors = lax.all_to_all(factors, "dap", 0, 0, axis_index_groups=[order])

    pair, scale, spread = call(
        prepare_kernel,
        (
            struct(couple_features.shape, F32),
            struct(couple_features.shape, F32),
            struct((width, width * channels), BF16),
        ),
        vmem(6),
        "prepare",
        16 * rows * size * channels,
        16 * rows * size * channels,
        [
            pltpu.VMEM((width * width, channels), F32),
            pltpu.VMEM((size, channels), F32),
            pltpu.VMEM((size, channels), F32),
        ],
    )(
        ids_row,
        amino_row,
        strand_couple_embedding,
        couple_features,
        alignment_presence,
        tensor_reduce_matrix,
    )

    refreshed = call(
        functools.partial(outer_kernel, order),
        struct(couple_features.shape, BF16),
        vmem(4),
        "outer_mean",
        4 * rows * size * channels * width * seqs * devices,
        16 * rows * size * channels,
        [
            pltpu.VMEM((blocks, width * devices, LANES), F32),
            pltpu.VMEM((seqs * rows * devices, LANES), F32),
        ],
    )(factors, spread, pair, scale)
    return (mixed, refreshed)


def solution(mesh):
    in_specs = (
        P(("cplx", "dap"), None, None),
        P(("cplx", "dap"), None, None),
        P("cplx", None),
        P("cplx"),
        P("cplx"),
        P(),
        P(),
        P(),
        P(),
        P(),
        P(),
    )
    out_specs = (P(("cplx", "dap"), None, None), P(("cplx", "dap"), None, None))
    return jax.shard_map(
        on_device, mesh=mesh, in_specs=in_specs, out_specs=out_specs, check_vma=False
    )
```

```python
import functools

import jax
import jax.numpy as jnp
from jax import lax
from jax.experimental import pallas as pl
from jax.experimental.pallas import tpu as pltpu
from jax.sharding import PartitionSpec as P

EPS = 1e-05
LANES = 128
F32 = jnp.float32
BF16 = jnp.bfloat16
VMEM_LIMIT = 24 * 1024 * 1024
VMEM_FULL = 63 * 1024 * 1024


def standardize(x):
    center = x - jnp.mean(x, axis=-1, keepdims=True)
    spread = jnp.mean(center * center, axis=-1, keepdims=True)
    return center * lax.rsqrt(spread + EPS)


def to_column(row, size):
    down = lax.broadcasted_iota(jnp.int32, (size, size), 0)
    across = lax.broadcasted_iota(jnp.int32, (size, size), 1)
    spread = jnp.where(down == across, jnp.broadcast_to(row, (size, size)), 0.0)
    return jnp.sum(spread, axis=1, keepdims=True)


def dot(a, b, contract):
    return lax.dot_general(a, b, (contract, ((), ())), preferred_element_type=F32)


NN = ((1,), (0,))
NT = ((1,), (1,))
TN = ((0,), (0,))


def pair_input(ids_row, emb, x, chains, res_start):
    rows, size, channels = x.shape
    chain = jnp.broadcast_to(to_column(ids_row[...].astype(F32), size), (size, channels))
    chains[...] = chain
    other, same = emb[0:1, :], emb[1:2, :]
    for i in range(rows):
        chain_i = chains[pl.ds(res_start + i, 1), :]
        yield x[i].astype(F32) + jnp.where(chain == chain_i, same, other)


def bias_kernel(ids_row, emb, x, logit, out, chains):
    rows, size, _ = x.shape
    heads = logit.shape[0]
    group = heads * rows
    pack = LANES // group
    part = size // pack
    res_start = lax.axis_index("dap") * rows
    head = lax.broadcasted_iota(jnp.int32, (heads, LANES), 0)
    lane = lax.broadcasted_iota(jnp.int32, (heads, LANES), 1)
    spread = jnp.where((lane % group) // rows == head, 1.0, 0.0).astype(BF16)
    wide = dot(logit[...], spread, TN).astype(BF16)
    normed = [standardize(z).astype(BF16) for z in pair_input(ids_row, emb, x, chains, res_start)]
    full = dot(jnp.concatenate(normed, axis=0), wide, NN)
    lane = lax.broadcasted_iota(jnp.int32, (part, LANES), 1)
    total = jnp.zeros((part, LANES), F32)
    for i in range(rows):
        for half in range(pack):
            begin = i * size + half * part
            pick = (lane // group == half) & (lane % rows == i)
            total = jnp.where(pick, full[begin : begin + part, :], total)
    total = total.astype(BF16)
    for peer in range(out.shape[0]):
        out[peer] = total


def prepare(ids_row, amino_row, emb, x, presence, reduce, pair, scale, spread, wide, chains, keeps):
    rows, size, channels = x.shape
    width = spread.shape[0]
    res_start = lax.axis_index("dap") * rows
    for i, z in enumerate(pair_input(ids_row, emb, x, chains, res_start)):
        pair[i] = z
    here = presence[...].astype(BF16)
    count = dot(here, here, TN)
    lane = lax.broadcasted_iota(jnp.int32, (size, size), 1)
    kept = jnp.broadcast_to(to_column(amino_row[...].astype(F32), size), (size, channels))
    keeps[...] = kept
    for i in range(rows):
        column = jnp.sum(jnp.where(lane == res_start + i, count, 0.0), axis=1, keepdims=True) + 1.0
        scale[i] = kept * keeps[pl.ds(res_start + i, 1), :] / column
    wide[...] = reduce[...].astype(F32)
    for e in range(width):
        spread[:, e * channels : (e + 1) * channels] = wide[pl.ds(e, width, stride=width), :].astype(BF16)


def project_kernel(
    x_far,
    weights_far,
    presence_far,
    ids_far,
    amino_far,
    emb_far,
    couple_far,
    reduce_far,
    scores,
    content,
    gate,
    present,
    present_row,
    pair,
    scale,
    spread,
    x,
    weights,
    presence,
    ids_row,
    amino_row,
    emb,
    couple,
    reduce,
    wide,
    chains,
    keeps,
    arrived,
):
    far = (x_far, weights_far, presence_far, ids_far, amino_far, emb_far, couple_far, reduce_far)
    near = (x, weights, presence, ids_row, amino_row, emb, couple, reduce)
    copies = [pltpu.make_async_copy(src, dst, arrived.at[n]) for n, (src, dst) in enumerate(zip(far, near))]
    for copy in copies:
        copy.start()
    copies[0].wait()
    seqs, size, depth = x.shape
    rows = couple.shape[0]
    merged = content.shape[2]
    group_total = scores.shape[2]
    heads = group_total // size
    head_size = merged // heads
    seq_start = lax.axis_index("dap") * seqs
    normed = standardize(x[...].reshape(seqs * size, depth).astype(F32)).astype(BF16)
    copies[1].wait()
    mapped = dot(normed, weights[...], NN)
    asking = (mapped[:, :merged] * head_size**-0.5).astype(BF16).astype(F32)
    target = mapped[:, merged : 2 * merged].astype(BF16)
    content[...] = mapped[:, 2 * merged : 3 * merged].astype(BF16).reshape(content.shape)
    gate[...] = jax.nn.sigmoid(mapped[:, 3 * merged :]).reshape(gate.shape)
    for copy in copies[2:]:
        copy.wait()
    lane = lax.broadcasted_iota(jnp.int32, (rows, merged), 1)
    row_pieces = []
    for s in range(seqs):
        pieces = []
        for begin in range(s * size, (s + 1) * size, rows):
            here = asking[begin : begin + rows, :]
            for h in range(heads):
                pieces.append(jnp.where(lane // head_size == h, here, 0.0))
        masked = jnp.concatenate(pieces, axis=0).astype(BF16)
        scores[s] = dot(target[s * size : (s + 1) * size, :], masked, NT)
        row = presence[pl.ds(seq_start + s, 1), :].astype(F32)
        present[s] = jnp.broadcast_to(to_column(row, size), (size, LANES))
        row_pieces.append(row)
    present_row[...] = jnp.concatenate(row_pieces, axis=1)
    prepare(ids_row, amino_row, emb, couple, presence, reduce, pair, scale, spread, wide, chains, keeps)


def attend_kernel(order, bias, scores, content, gate, present, present_row, x, merge, twin, mixed, out):
    devices, part, _ = bias.shape
    seqs, size, depth = x.shape
    merged = content.shape[2]
    pack = size // part
    group = LANES // pack
    rows = size // devices
    heads = group // rows
    head_size = merged // heads
    width = twin.shape[0] // 2
    lane = lax.broadcasted_iota(jnp.int32, (rows, merged), 1)
    gated = []
    tables = []
    for block in range(devices // pack):
        got = [bias[order.index(block * pack + n)].astype(F32) for n in range(pack)]
        tables.append(
            jnp.concatenate(
                [
                    jnp.concatenate([g[:, half * group : (half + 1) * group] for g in got], axis=1)
                    for half in range(pack)
                ],
                axis=0,
            )
        )
    for s in range(seqs):
        absent = (present[s] - 1.0) * 1000000000.0
        context = []
        for block in range(devices // pack):
            logits = scores[s, :, block * LANES : (block + 1) * LANES] + tables[block] + absent
            raised = jnp.exp(logits - jnp.max(logits, axis=0, keepdims=True))
            weights = raised * (1.0 / jnp.sum(raised, axis=0, keepdims=True))
            mixed_heads = dot(weights.astype(BF16), content[s], TN)
            for n in range(pack):
                total = jnp.zeros((rows, merged), F32)
                for h in range(heads):
                    begin = n * group + h * rows
                    total = jnp.where(lane // head_size == h, mixed_heads[begin : begin + rows, :], total)
                context.append(total)
        gated.append((gate[s] * jnp.concatenate(context, axis=0)).astype(BF16))
    offset = dot(jnp.concatenate(gated, axis=0), merge[...], NN)
    updated = (x[...].reshape(seqs * size, depth).astype(F32) + offset).astype(BF16)
    mixed[...] = updated.reshape(mixed.shape)
    normed = standardize(updated.astype(F32)).astype(BF16)
    left = dot(normed, twin[...], NT)
    right = (dot(twin[width:, :], normed, NT) * present_row[...]).astype(BF16)
    blocks = seqs * size // LANES
    for peer in range(devices):
        for block in range(blocks):
            out[peer, block * width : (block + 1) * width, :] = right[:, block * LANES : (block + 1) * LANES]
    for slot, peer in enumerate(order):
        rows_here = []
        for s in range(seqs):
            begin = peer * rows
            here = left[s * size + begin : s * size + begin + rows, :]
            rows_here.append(here * present[s, begin : begin + rows, : 2 * width])
        piece = jnp.concatenate(rows_here, axis=0)
        piece = jnp.concatenate([piece, jnp.zeros((seqs * rows, LANES - 2 * width), F32)], axis=1)
        out[slot, blocks * width :, :] = piece.astype(BF16)


def outer_kernel(order, got, spread, pair, scale, mixed, out, mixed_out, right_rows, left_rows, done):
    keep = pltpu.make_async_copy(mixed, mixed_out, done)
    keep.start()
    devices = got.shape[0]
    rows, size, channels = pair.shape
    width = spread.shape[0]
    blocks = right_rows.shape[0]
    seqs = blocks * LANES // size
    for slot, peer in enumerate(order):
        for block in range(blocks):
            right_rows[block, pl.ds(peer, width, stride=devices), :] = got[
                slot, block * width : (block + 1) * width, :
            ].astype(F32)
        left_rows[pl.ds(peer, seqs * rows, stride=devices), :] = got[slot, blocks * width :, :].astype(F32)
    right = jnp.concatenate([jnp.transpose(right_rows[block]) for block in range(blocks)], axis=0).astype(BF16)
    left = left_rows[...][:, :width].astype(BF16)
    table = dot(left, spread[...], NN)
    for i in range(rows):
        update = jnp.zeros((size, channels), F32)
        for s in range(seqs):
            begin = (s * rows + i) * devices
            columns = jnp.concatenate(
                [table[begin : begin + devices, e * channels : (e + 1) * channels] for e in range(width)], axis=0
            ).astype(BF16)
            update = update + dot(right[s * size : (s + 1) * size, :], columns, NN)
        out[i] = (pair[i] + scale[i] * update).astype(BF16)
    keep.wait()


def member_order(devices):
    return [(5 * devices // 8 - n) % devices for n in range(devices)]


def vmem(count):
    return [pl.BlockSpec(memory_space=pltpu.VMEM) for _ in range(count)]


def call(body, shapes, in_specs, name, flops, moved, scratch=(), limit=VMEM_LIMIT):
    return pl.pallas_call(
        body,
        out_shape=shapes,
        in_specs=in_specs,
        out_specs=jax.tree.map(lambda _: pl.BlockSpec(memory_space=pltpu.VMEM), shapes),
        scratch_shapes=list(scratch),
        compiler_params=pltpu.CompilerParams(vmem_limit_bytes=limit),
        cost_estimate=pl.CostEstimate(flops=flops, bytes_accessed=moved, transcendentals=0),
        name=name,
    )


def on_device(
    alignment_features,
    couple_features,
    alignment_presence,
    amino_presence,
    strand_identity,
    strand_couple_embedding,
    fourfold_input_matrix,
    heads_merge_matrix,
    couple_logit_matrix,
    twin_factor_matrix,
    tensor_reduce_matrix,
):
    rows, size, channels = couple_features.shape
    seqs, _, depth = alignment_features.shape
    devices = size // rows
    heads = couple_logit_matrix.shape[1]
    merged = heads_merge_matrix.shape[0]
    width = twin_factor_matrix.shape[1] // 2
    group = heads * rows
    pack = LANES // group
    struct = jax.ShapeDtypeStruct
    order = member_order(devices)
    ids_row = strand_identity.reshape(1, size)
    amino_row = amino_presence.reshape(1, size)

    bias = call(
        bias_kernel,
        struct((devices, size // pack, LANES), BF16),
        vmem(4),
        "pair_bias",
        2 * rows * size * channels * LANES,
        2 * rows * size * channels,
        [pltpu.VMEM((size, channels), F32)],
        VMEM_FULL,
    )(ids_row, strand_couple_embedding, couple_features, couple_logit_matrix.T)
    bias = lax.all_to_all(bias, "dap", 0, 0, axis_index_groups=[order])

    project_inputs = (
        alignment_features,
        fourfold_input_matrix,
        alignment_presence,
        ids_row,
        amino_row,
        strand_couple_embedding,
        couple_features,
        tensor_reduce_matrix,
    )
    scores, content, gate, present, present_row, pair, scale, spread = call(
        project_kernel,
        (
            struct((seqs, size, heads * size), F32),
            struct((seqs, size, merged), BF16),
            struct((seqs, size, merged), F32),
            struct((seqs, size, LANES), F32),
            struct((1, seqs * size), F32),
            struct(couple_features.shape, F32),
            struct(couple_features.shape, F32),
            struct((width, width * channels), BF16),
        ),
        [pl.BlockSpec(memory_space=pltpu.HBM)] * 8,
        "project",
        2 * seqs * size * depth * 4 * merged + 2 * seqs * size * size * heads * merged,
        2 * depth * 4 * merged,
        [pltpu.VMEM(array.shape, array.dtype) for array in project_inputs]
        + [
            pltpu.VMEM((width * width, channels), F32),
            pltpu.VMEM((size, channels), F32),
            pltpu.VMEM((size, channels), F32),
            pltpu.SemaphoreType.DMA((len(project_inputs),)),
        ],
    )(*[pltpu.with_memory_space_constraint(array, pltpu.HBM) for array in project_inputs])

    blocks = seqs * size // LANES
    mixed, factors = call(
        functools.partial(attend_kernel, order),
        (
            pltpu.VMEM(alignment_features.shape, BF16),
            struct((devices, blocks * width + seqs * rows, LANES), BF16),
        ),
        vmem(9),
        "attend",
        4 * seqs * size * size * heads * merged,
        8 * seqs * size * size * heads,
    )(
        bias,
        scores,
        content,
        gate,
        present,
        present_row,
        alignment_features,
        heads_merge_matrix,
        twin_factor_matrix.T,
    )
    factors = lax.all_to_all(factors, "dap", 0, 0, axis_index_groups=[order])

    refreshed, mixed = pl.pallas_call(
        functools.partial(outer_kernel, order),
        out_shape=(struct(couple_features.shape, BF16), struct(alignment_features.shape, BF16)),
        in_specs=vmem(5),
        out_specs=(pl.BlockSpec(memory_space=pltpu.VMEM), pl.BlockSpec(memory_space=pl.ANY)),
        scratch_shapes=[
            pltpu.VMEM((blocks, width * devices, LANES), F32),
            pltpu.VMEM((seqs * rows * devices, LANES), F32),
            pltpu.SemaphoreType.DMA,
        ],
        compiler_params=pltpu.CompilerParams(vmem_limit_bytes=VMEM_LIMIT),
        cost_estimate=pl.CostEstimate(
            flops=4 * rows * size * channels * width * seqs * devices,
            bytes_accessed=16 * rows * size * channels,
            transcendentals=0,
        ),
        name="outer_mean",
    )(factors, spread, pair, scale, mixed)
    return (mixed, refreshed)


def solution(mesh):
    in_specs = (
        P(("cplx", "dap"), None, None),
        P(("cplx", "dap"), None, None),
        P("cplx", None),
        P("cplx"),
        P("cplx"),
        P(),
        P(),
        P(),
        P(),
        P(),
        P(),
    )
    out_specs = (P(("cplx", "dap"), None, None), P(("cplx", "dap"), None, None))
    return jax.shard_map(
        on_device, mesh=mesh, in_specs=in_specs, out_specs=out_specs, check_vma=False
    )
```

```python
import functools
import math

import jax
import jax.numpy as jnp
from jax import lax
from jax.experimental import pallas as pl
from jax.experimental.pallas import tpu as pltpu
from jax.sharding import PartitionSpec as P

EPS = 1e-05
LANES = 128
F32 = jnp.float32
BF16 = jnp.bfloat16
VMEM_LIMIT = 24 * 1024 * 1024
GROUPS = 8
PAIR = 2
VMEM_FULL = 63 * 1024 * 1024


def standardize(x):
    center = x - jnp.mean(x, axis=-1, keepdims=True)
    spread = jnp.mean(center * center, axis=-1, keepdims=True)
    return center * lax.rsqrt(spread + EPS)


def to_column(row, size):
    down = lax.broadcasted_iota(jnp.int32, (size, size), 0)
    across = lax.broadcasted_iota(jnp.int32, (size, size), 1)
    spread = jnp.where(down == across, jnp.broadcast_to(row, (size, size)), 0.0)
    return jnp.sum(spread, axis=1, keepdims=True)


def dot(a, b, contract):
    return lax.dot_general(a, b, (contract, ((), ())), preferred_element_type=F32)


NN = ((1,), (0,))
NT = ((1,), (1,))
TN = ((0,), (0,))


def pair_input(ids_row, emb, x, chains, res_start):
    rows, size, channels = x.shape
    chain = jnp.broadcast_to(to_column(ids_row[...].astype(F32), size), (size, channels))
    chains[...] = chain
    other, same = emb[0:1, :], emb[1:2, :]
    for i in range(rows):
        chain_i = chains[pl.ds(res_start + i, 1), :]
        yield x[i].astype(F32) + jnp.where(chain == chain_i, same, other)


def bias_kernel(ids_row, emb, x, logit, out, chains):
    rows, size, _ = x.shape
    heads = logit.shape[0]
    group = heads * rows
    pack = LANES // group
    part = size // pack
    res_start = lax.axis_index("dap") * rows
    head = lax.broadcasted_iota(jnp.int32, (heads, LANES), 0)
    lane = lax.broadcasted_iota(jnp.int32, (heads, LANES), 1)
    spread = jnp.where((lane % group) // rows == head, 1.0, 0.0).astype(BF16)
    wide = dot(logit[...], spread, TN).astype(BF16)
    normed = [standardize(z).astype(BF16) for z in pair_input(ids_row, emb, x, chains, res_start)]
    full = dot(jnp.concatenate(normed, axis=0), wide, NN)
    lane = lax.broadcasted_iota(jnp.int32, (part, LANES), 1)
    total = jnp.zeros((part, LANES), F32)
    for i in range(rows):
        for half in range(pack):
            begin = i * size + half * part
            pick = (lane // group == half) & (lane % rows == i)
            total = jnp.where(pick, full[begin : begin + part, :], total)
    total = total.astype(BF16)
    for peer in range(out.shape[0]):
        out[peer] = total


def prepare(ids_row, amino_row, emb, x, presence, reduce, pair, scale, spread, wide, chains, keeps):
    rows, size, channels = x.shape
    width = spread.shape[0] // GROUPS
    res_start = lax.axis_index("dap") * rows
    for i, z in enumerate(pair_input(ids_row, emb, x, chains, res_start)):
        pair[i] = z
    here = presence[...].astype(BF16)
    count = dot(here, here, TN)
    lane = lax.broadcasted_iota(jnp.int32, (size, size), 1)
    kept = jnp.broadcast_to(to_column(amino_row[...].astype(F32), size), (size, channels))
    keeps[...] = kept
    for i in range(rows):
        column = jnp.sum(jnp.where(lane == res_start + i, count, 0.0), axis=1, keepdims=True) + 1.0
        scale[i] = kept * keeps[pl.ds(res_start + i, 1), :] / column
    wide[...] = reduce[...].astype(F32)
    each = width // GROUPS
    for e in range(width):
        group, place = e // each, e % each
        spread[group * width : (group + 1) * width, place * channels : (place + 1) * channels] = wide[
            pl.ds(e, width, stride=width), :
        ].astype(BF16)


def project_kernel(
    x_far,
    weights_far,
    presence_far,
    ids_far,
    amino_far,
    emb_far,
    couple_far,
    reduce_far,
    scores,
    content,
    gate,
    present,
    present_row,
    pair,
    scale,
    spread,
    x,
    weights,
    presence,
    ids_row,
    amino_row,
    emb,
    couple,
    reduce,
    wide,
    chains,
    keeps,
    arrived,
):
    far = (x_far, weights_far, presence_far, ids_far, amino_far, emb_far, couple_far, reduce_far)
    near = (x, weights, presence, ids_row, amino_row, emb, couple, reduce)
    copies = [pltpu.make_async_copy(src, dst, arrived.at[n]) for n, (src, dst) in enumerate(zip(far, near))]
    for copy in copies:
        copy.start()
    copies[0].wait()
    seqs, size, depth = x.shape
    rows = couple.shape[0]
    merged = content.shape[2]
    group_total = scores.shape[2]
    heads = group_total // size
    head_size = merged // heads
    seq_start = lax.axis_index("dap") * seqs
    normed = standardize(x[...].reshape(seqs * size, depth).astype(F32)).astype(BF16)
    copies[1].wait()
    mapped = dot(normed, weights[...], NN)
    asking = (mapped[:, :merged] * head_size**-0.5).astype(BF16).astype(F32)
    target = mapped[:, merged : 2 * merged].astype(BF16)
    content[...] = mapped[:, 2 * merged : 3 * merged].astype(BF16).reshape(content.shape)
    gate[...] = jax.nn.sigmoid(mapped[:, 3 * merged :]).reshape(gate.shape)
    for copy in copies[2:]:
        copy.wait()
    lane = lax.broadcasted_iota(jnp.int32, (rows, merged), 1)
    row_pieces = []
    for s in range(seqs):
        pieces = []
        for begin in range(s * size, (s + 1) * size, rows):
            here = asking[begin : begin + rows, :]
            for h in range(heads):
                pieces.append(jnp.where(lane // head_size == h, here, 0.0))
        masked = jnp.concatenate(pieces, axis=0).astype(BF16)
        scores[s] = dot(target[s * size : (s + 1) * size, :], masked, NT)
        row = presence[pl.ds(seq_start + s, 1), :].astype(F32)
        present[s] = jnp.broadcast_to(to_column(row, size), (size, LANES))
        row_pieces.append(row)
    present_row[...] = jnp.concatenate(row_pieces, axis=1)
    prepare(ids_row, amino_row, emb, couple, presence, reduce, pair, scale, spread, wide, chains, keeps)


def attend_kernel(order, bias, scores, content, gate, present, present_row, x, merge, twin, mixed, out):
    devices, part, _ = bias.shape
    seqs, size, depth = x.shape
    merged = content.shape[2]
    pack = size // part
    group = LANES // pack
    rows = size // devices
    heads = group // rows
    head_size = merged // heads
    width = twin.shape[0] // 2
    lane = lax.broadcasted_iota(jnp.int32, (rows, LANES), 1)
    gated = []
    tables = []
    for block in range(devices // pack):
        got = [bias[order.index(block * pack + n)].astype(F32) for n in range(pack)]
        tables.append(
            jnp.concatenate(
                [
                    jnp.concatenate([g[:, half * group : (half + 1) * group] for g in got], axis=1)
                    for half in range(pack)
                ],
                axis=0,
            )
        )
    tiles = merged // LANES
    few = heads // tiles
    for s in range(seqs):
        absent = (present[s] - 1.0) * 1000000000.0
        turned = []
        for block in range(devices // pack):
            logits = scores[s, :, block * LANES : (block + 1) * LANES] + tables[block] + absent
            raised = jnp.exp(logits - jnp.max(logits, axis=0, keepdims=True))
            weights = raised * (1.0 / jnp.sum(raised, axis=0, keepdims=True))
            turned.append(jnp.transpose(weights.astype(BF16)))
        context = []
        for tile in range(tiles):
            mine = []
            for block in range(devices // pack):
                for n in range(pack):
                    begin = n * group + tile * few * rows
                    mine.append(turned[block][begin : begin + few * rows, :])
            product = dot(jnp.concatenate(mine, axis=0), content[s, :, tile * LANES : (tile + 1) * LANES], NN)
            picked = []
            for peer in range(devices):
                total = product[peer * few * rows : peer * few * rows + rows, :]
                for h in range(1, few):
                    begin = (peer * few + h) * rows
                    total = jnp.where(lane // head_size == h, product[begin : begin + rows, :], total)
                picked.append(total)
            context.append(jnp.concatenate(picked, axis=0))
        gated.append((gate[s] * jnp.concatenate(context, axis=1)).astype(BF16))
    offset = dot(jnp.concatenate(gated, axis=0), merge[...], NN)
    updated = (x[...].reshape(seqs * size, depth).astype(F32) + offset).astype(BF16)
    mixed[...] = updated.reshape(mixed.shape)
    normed = standardize(updated.astype(F32)).astype(BF16)
    left = dot(normed, jnp.concatenate([twin[:width, :]] * (LANES // width), axis=0), NT)
    right = (dot(twin[width:, :], normed, NT) * present_row[...]).astype(BF16)
    blocks = seqs * size // LANES
    for peer in range(devices):
        for block in range(blocks):
            out[peer, block * width : (block + 1) * width, :] = right[:, block * LANES : (block + 1) * LANES]
    for slot, peer in enumerate(order):
        rows_here = []
        for s in range(seqs):
            begin = peer * rows
            here = left[s * size + begin : s * size + begin + rows, :]
            rows_here.append(here * present[s, begin : begin + rows, :])
        out[slot, blocks * width :, :] = jnp.concatenate(rows_here, axis=0).astype(BF16)


def outer_kernel(order, got, spread, pair, scale, mixed, out_far, mixed_out, right_rows, left_rows, out, done):
    keep = [pltpu.make_async_copy(mixed, mixed_out, done.at[0])]
    keep[0].start()
    devices = got.shape[0]
    rows, size, channels = pair.shape
    width = math.isqrt(spread.shape[0] * spread.shape[1] // channels)
    groups = spread.shape[0] // width
    blocks = right_rows.shape[0]
    seqs = blocks * LANES // size
    for slot, peer in enumerate(order):
        for block in range(blocks):
            right_rows[block, pl.ds(peer, width, stride=devices), :] = got[
                slot, block * width : (block + 1) * width, :
            ].astype(F32)
        left_rows[pl.ds(peer, seqs * rows, stride=devices), :] = got[slot, blocks * width :, :].astype(F32)
    right = jnp.concatenate([jnp.transpose(right_rows[block]) for block in range(blocks)], axis=0).astype(BF16)
    copies = LANES // width
    tiles = groups // copies
    lane = lax.broadcasted_iota(jnp.int32, (seqs * PAIR * devices, LANES), 1)
    blank = jnp.zeros((seqs * PAIR * devices, LANES), BF16)
    pieces = []
    for first in range(0, rows, PAIR):
        begins = [(s * rows + first + i) * devices for s in range(seqs) for i in range(PAIR)]
        left = jnp.concatenate([left_rows[begin : begin + devices, :] for begin in begins], axis=0)
        for group in range(groups):
            mine = jnp.where(lane // width == group % copies, left, 0.0).astype(BF16)
            pieces.append(jnp.concatenate([mine if n == group // copies else blank for n in range(tiles)], axis=1))
    table = dot(jnp.concatenate(pieces, axis=0), spread[...], NN)
    for first in range(0, rows, PAIR):
        update = jnp.zeros((size, PAIR * channels), F32)
        for s in range(seqs):
            columns = []
            for i in range(PAIR):
                column = []
                for e in range(width):
                    group, place = e // (width // groups), e % (width // groups)
                    begin = ((first // PAIR * groups + group) * seqs * PAIR + s * PAIR + i) * devices
                    column.append(table[begin : begin + devices, place * channels : (place + 1) * channels])
                columns.append(jnp.concatenate(column, axis=0).astype(BF16))
            columns = jnp.concatenate(columns, axis=1)
            update = update + dot(right[s * size : (s + 1) * size, :], columns, NN)
        for i in range(PAIR):
            here = update[:, i * channels : (i + 1) * channels]
            out[first + i] = (pair[first + i] + scale[first + i] * here).astype(BF16)
        ready = pl.ds(first, PAIR)
        keep.append(pltpu.make_async_copy(out.at[ready], out_far.at[ready], done.at[1 + first // PAIR]))
        keep[-1].start()
    for copy in keep:
        copy.wait()


def member_order(devices):
    return [(5 * devices // 8 - n) % devices for n in range(devices)]


def vmem(count):
    return [pl.BlockSpec(memory_space=pltpu.VMEM) for _ in range(count)]


def call(body, shapes, in_specs, name, flops, moved, scratch=(), limit=VMEM_LIMIT):
    return pl.pallas_call(
        body,
        out_shape=shapes,
        in_specs=in_specs,
        out_specs=jax.tree.map(lambda _: pl.BlockSpec(memory_space=pltpu.VMEM), shapes),
        scratch_shapes=list(scratch),
        compiler_params=pltpu.CompilerParams(vmem_limit_bytes=limit),
        cost_estimate=pl.CostEstimate(flops=flops, bytes_accessed=moved, transcendentals=0),
        name=name,
    )


def on_device(
    alignment_features,
    couple_features,
    alignment_presence,
    amino_presence,
    strand_identity,
    strand_couple_embedding,
    fourfold_input_matrix,
    heads_merge_matrix,
    couple_logit_matrix,
    twin_factor_matrix,
    tensor_reduce_matrix,
):
    rows, size, channels = couple_features.shape
    seqs, _, depth = alignment_features.shape
    devices = size // rows
    heads = couple_logit_matrix.shape[1]
    merged = heads_merge_matrix.shape[0]
    width = twin_factor_matrix.shape[1] // 2
    group = heads * rows
    pack = LANES // group
    struct = jax.ShapeDtypeStruct
    order = member_order(devices)
    ids_row = strand_identity.reshape(1, size)
    amino_row = amino_presence.reshape(1, size)

    bias = call(
        bias_kernel,
        struct((devices, size // pack, LANES), BF16),
        vmem(4),
        "pair_bias",
        2 * rows * size * channels * LANES,
        2 * rows * size * channels,
        [pltpu.VMEM((size, channels), F32)],
        VMEM_FULL,
    )(ids_row, strand_couple_embedding, couple_features, couple_logit_matrix.T)
    bias = lax.all_to_all(bias, "dap", 0, 0, axis_index_groups=[order])

    project_inputs = (
        alignment_features,
        fourfold_input_matrix,
        alignment_presence,
        ids_row,
        amino_row,
        strand_couple_embedding,
        couple_features,
        tensor_reduce_matrix,
    )
    scores, content, gate, present, present_row, pair, scale, spread = call(
        project_kernel,
        (
            struct((seqs, size, heads * size), F32),
            struct((seqs, size, merged), BF16),
            struct((seqs, size, merged), F32),
            struct((seqs, size, LANES), F32),
            struct((1, seqs * size), F32),
            struct(couple_features.shape, F32),
            struct(couple_features.shape, F32),
            struct((GROUPS * width, width // GROUPS * channels), BF16),
        ),
        [pl.BlockSpec(memory_space=pltpu.HBM)] * 8,
        "project",
        2 * seqs * size * depth * 4 * merged + 2 * seqs * size * size * heads * merged,
        2 * depth * 4 * merged,
        [pltpu.VMEM(array.shape, array.dtype) for array in project_inputs]
        + [
            pltpu.VMEM((width * width, channels), F32),
            pltpu.VMEM((size, channels), F32),
            pltpu.VMEM((size, channels), F32),
            pltpu.SemaphoreType.DMA((len(project_inputs),)),
        ],
    )(*[pltpu.with_memory_space_constraint(array, pltpu.HBM) for array in project_inputs])

    blocks = seqs * size // LANES
    mixed, factors = call(
        functools.partial(attend_kernel, order),
        (
            pltpu.VMEM(alignment_features.shape, BF16),
            struct((devices, blocks * width + seqs * rows, LANES), BF16),
        ),
        vmem(9),
        "attend",
        4 * seqs * size * size * heads * merged,
        8 * seqs * size * size * heads,
    )(
        bias,
        scores,
        content,
        gate,
        present,
        present_row,
        alignment_features,
        heads_merge_matrix,
        twin_factor_matrix.T,
    )
    factors = lax.all_to_all(factors, "dap", 0, 0, axis_index_groups=[order])

    refreshed, mixed = pl.pallas_call(
        functools.partial(outer_kernel, order),
        out_shape=(struct(couple_features.shape, BF16), struct(alignment_features.shape, BF16)),
        in_specs=vmem(5),
        out_specs=(pl.BlockSpec(memory_space=pl.ANY), pl.BlockSpec(memory_space=pl.ANY)),
        scratch_shapes=[
            pltpu.VMEM((blocks, width * devices, LANES), F32),
            pltpu.VMEM((seqs * rows * devices, LANES), F32),
            pltpu.VMEM(couple_features.shape, BF16),
            pltpu.SemaphoreType.DMA((1 + rows // PAIR,)),
        ],
        compiler_params=pltpu.CompilerParams(vmem_limit_bytes=VMEM_LIMIT),
        cost_estimate=pl.CostEstimate(
            flops=4 * rows * size * channels * width * seqs * devices,
            bytes_accessed=16 * rows * size * channels,
            transcendentals=0,
        ),
        name="outer_mean",
    )(factors, spread, pair, scale, mixed)
    return (mixed, refreshed)


def solution(mesh):
    in_specs = (
        P(("cplx", "dap"), None, None),
        P(("cplx", "dap"), None, None),
        P("cplx", None),
        P("cplx"),
        P("cplx"),
        P(),
        P(),
        P(),
        P(),
        P(),
        P(),
    )
    out_specs = (P(("cplx", "dap"), None, None), P(("cplx", "dap"), None, None))
    return jax.shard_map(
        on_device, mesh=mesh, in_specs=in_specs, out_specs=out_specs, check_vma=False
    )
```

```python
import functools
import math

import jax
import jax.numpy as jnp
from jax import lax
from jax.experimental import pallas as pl
from jax.experimental.pallas import tpu as pltpu
from jax.sharding import PartitionSpec as P

EPS = 1e-05
LANES = 128
F32 = jnp.float32
BF16 = jnp.bfloat16
VMEM_LIMIT = 24 * 1024 * 1024
GROUPS = 8
PAIR = 2
VMEM_FULL = 63 * 1024 * 1024


def standardize(x):
    center = x - jnp.mean(x, axis=-1, keepdims=True)
    spread = jnp.mean(center * center, axis=-1, keepdims=True)
    return center * lax.rsqrt(spread + EPS)


def to_column(row, size):
    down = lax.broadcasted_iota(jnp.int32, (size, size), 0)
    across = lax.broadcasted_iota(jnp.int32, (size, size), 1)
    spread = jnp.where(down == across, jnp.broadcast_to(row, (size, size)), 0.0)
    return jnp.sum(spread, axis=1, keepdims=True)


def dot(a, b, contract):
    return lax.dot_general(a, b, (contract, ((), ())), preferred_element_type=F32)


NN = ((1,), (0,))
NT = ((1,), (1,))
TN = ((0,), (0,))


def pair_input(ids_row, emb, x, chains, res_start):
    rows, size, channels = x.shape
    chain = jnp.broadcast_to(to_column(ids_row[...].astype(F32), size), (size, channels))
    chains[...] = chain
    other, same = emb[0:1, :], emb[1:2, :]
    for i in range(rows):
        chain_i = chains[pl.ds(res_start + i, 1), :]
        yield x[i].astype(F32) + jnp.where(chain == chain_i, same, other)


def bias_kernel(*refs):
    count = (len(refs) - 3) // 2
    far, out, near = refs[:count], refs[count], refs[count + 1 : 2 * count]
    logit, chains, arrived = refs[-3:]
    x, ids_row, emb = near[:3]
    near = (x, logit, ids_row, emb) + near[3:]
    rows, size, _ = x.shape
    each = max(1, rows // 4)
    moves = [(far[0].at[pl.ds(b, each)], x.at[pl.ds(b, each)]) for b in range(0, rows, each)]
    first = len(moves) + 3
    moves += list(zip(far[1:], near[1:]))
    copies = [pltpu.make_async_copy(src, dst, arrived.at[n]) for n, (src, dst) in enumerate(moves)]
    for copy in copies:
        copy.start()
    for copy in copies[:first]:
        copy.wait()
    heads = logit.shape[0]
    group = heads * rows
    pack = LANES // group
    part = size // pack
    res_start = lax.axis_index("dap") * rows
    table = logit[...].astype(F32)
    wide = [jnp.broadcast_to(table[h : h + 1, :], (rows, table.shape[1])) for h in range(heads)] * pack
    wide = jnp.concatenate(wide, axis=0).astype(BF16)
    normed = [standardize(z).astype(BF16) for z in pair_input(ids_row, emb, x, chains, res_start)]
    full = dot(jnp.concatenate(normed, axis=0), wide, NT)
    lane = lax.broadcasted_iota(jnp.int32, (part, LANES), 1)
    total = jnp.zeros((part, LANES), F32)
    for i in range(rows):
        for half in range(pack):
            begin = i * size + half * part
            pick = (lane // group == half) & (lane % rows == i)
            total = jnp.where(pick, full[begin : begin + part, :], total)
    total = total.astype(BF16)
    for peer in range(out.shape[0]):
        out[peer] = total
    for copy in copies[first:]:
        copy.wait()


def prepare(ids_row, amino_row, emb, x, presence, reduce, pair, scale, spread, wide, chains, keeps):
    rows, size, channels = x.shape
    width = spread.shape[0] // GROUPS
    res_start = lax.axis_index("dap") * rows
    for i, z in enumerate(pair_input(ids_row, emb, x, chains, res_start)):
        pair[i] = z
    here = presence[...].astype(BF16)
    count = dot(here, here, TN)
    lane = lax.broadcasted_iota(jnp.int32, (size, size), 1)
    kept = jnp.broadcast_to(to_column(amino_row[...].astype(F32), size), (size, channels))
    keeps[...] = kept
    for i in range(rows):
        column = jnp.sum(jnp.where(lane == res_start + i, count, 0.0), axis=1, keepdims=True) + 1.0
        scale[i] = kept * keeps[pl.ds(res_start + i, 1), :] / column
    wide[...] = reduce[...].astype(F32)
    each = width // GROUPS
    for e in range(width):
        group, place = e // each, e % each
        spread[group * width : (group + 1) * width, place * channels : (place + 1) * channels] = wide[
            pl.ds(e, width, stride=width), :
        ].astype(BF16)


def project(
    x,
    weights,
    presence,
    ids_row,
    amino_row,
    emb,
    couple,
    reduce,
    scores,
    content,
    gate,
    present,
    present_row,
    pair,
    scale,
    spread,
    wide,
    chains,
    keeps,
):
    seqs, size, depth = x.shape
    rows = couple.shape[0]
    merged = content.shape[2]
    group_total = scores.shape[2]
    heads = group_total // size
    head_size = merged // heads
    seq_start = lax.axis_index("dap") * seqs
    normed = standardize(x[...].reshape(seqs * size, depth).astype(F32)).astype(BF16)
    mapped = dot(normed, weights[...], NN)
    asking = (mapped[:, :merged] * head_size**-0.5).astype(BF16).astype(F32)
    target = mapped[:, merged : 2 * merged].astype(BF16)
    content[...] = mapped[:, 2 * merged : 3 * merged].astype(BF16).reshape(content.shape)
    gate[...] = jax.nn.sigmoid(mapped[:, 3 * merged :]).reshape(gate.shape)
    lane = lax.broadcasted_iota(jnp.int32, (rows, merged), 1)
    row_pieces = []
    for s in range(seqs):
        pieces = []
        for begin in range(s * size, (s + 1) * size, rows):
            here = asking[begin : begin + rows, :]
            for h in range(heads):
                pieces.append(jnp.where(lane // head_size == h, here, 0.0))
        masked = jnp.concatenate(pieces, axis=0).astype(BF16)
        scores[s] = dot(target[s * size : (s + 1) * size, :], masked, NT)
        row = presence[pl.ds(seq_start + s, 1), :].astype(F32)
        present[s] = jnp.broadcast_to(to_column(row, size), (size, LANES))
        row_pieces.append(row)
    present_row[...] = jnp.concatenate(row_pieces, axis=1)
    prepare(ids_row, amino_row, emb, couple, presence, reduce, pair, scale, spread, wide, chains, keeps)


def attend(order, bias, scores, content, gate, present, present_row, x, merge, twin, mixed, out):
    devices, part, _ = bias.shape
    seqs, size, depth = x.shape
    merged = content.shape[2]
    pack = size // part
    group = LANES // pack
    rows = size // devices
    heads = group // rows
    head_size = merged // heads
    width = twin.shape[0] // 2
    lane = lax.broadcasted_iota(jnp.int32, (rows, LANES), 1)
    gated = []
    tables = []
    for block in range(devices // pack):
        got = [bias[order.index(block * pack + n)].astype(F32) for n in range(pack)]
        tables.append(
            jnp.concatenate(
                [
                    jnp.concatenate([g[:, half * group : (half + 1) * group] for g in got], axis=1)
                    for half in range(pack)
                ],
                axis=0,
            )
        )
    tiles = merged // LANES
    few = heads // tiles
    for s in range(seqs):
        absent = (present[s] - 1.0) * 1000000000.0
        turned = []
        for block in range(devices // pack):
            logits = scores[s, :, block * LANES : (block + 1) * LANES] + tables[block] + absent
            raised = jnp.exp(logits - jnp.max(logits, axis=0, keepdims=True))
            weights = raised * (1.0 / jnp.sum(raised, axis=0, keepdims=True))
            turned.append(jnp.transpose(weights.astype(BF16)))
        context = []
        for tile in range(tiles):
            mine = []
            for block in range(devices // pack):
                for n in range(pack):
                    begin = n * group + tile * few * rows
                    mine.append(turned[block][begin : begin + few * rows, :])
            product = dot(jnp.concatenate(mine, axis=0), content[s, :, tile * LANES : (tile + 1) * LANES], NN)
            picked = []
            for peer in range(devices):
                total = product[peer * few * rows : peer * few * rows + rows, :]
                for h in range(1, few):
                    begin = (peer * few + h) * rows
                    total = jnp.where(lane // head_size == h, product[begin : begin + rows, :], total)
                picked.append(total)
            context.append(jnp.concatenate(picked, axis=0))
        gated.append((gate[s] * jnp.concatenate(context, axis=1)).astype(BF16))
    offset = dot(jnp.concatenate(gated, axis=0), merge[...], NN)
    updated = (x[...].reshape(seqs * size, depth).astype(F32) + offset).astype(BF16)
    mixed[...] = updated.reshape(mixed.shape)
    normed = standardize(updated.astype(F32)).astype(BF16)
    left = dot(normed, jnp.concatenate([twin[:width, :]] * (LANES // width), axis=0), NT)
    right = (dot(twin[width:, :], normed, NT) * present_row[...]).astype(BF16)
    blocks = seqs * size // LANES
    for peer in range(devices):
        for block in range(blocks):
            out[peer, block * width : (block + 1) * width, :] = right[:, block * LANES : (block + 1) * LANES]
    for slot, peer in enumerate(order):
        rows_here = []
        for s in range(seqs):
            begin = peer * rows
            here = left[s * size + begin : s * size + begin + rows, :]
            rows_here.append(here * present[s, begin : begin + rows, :])
        out[slot, blocks * width :, :] = jnp.concatenate(rows_here, axis=0).astype(BF16)


def middle_kernel(
    order,
    bias,
    x,
    weights,
    presence,
    ids_row,
    amino_row,
    emb,
    couple,
    reduce,
    merge,
    twin,
    mixed,
    out,
    pair,
    scale,
    spread,
    scores,
    content,
    gate,
    present,
    present_row,
    wide,
    chains,
    keeps,
):
    kept = (scores, content, gate, present, present_row)
    project(
        x, weights, presence, ids_row, amino_row, emb, couple, reduce, *kept, pair, scale, spread, wide, chains, keeps
    )
    attend(order, bias, *kept, x, merge, twin, mixed, out)


def outer_kernel(order, got, spread, pair, scale, mixed, out_far, mixed_out, right_rows, left_rows, out, done):
    keep = [pltpu.make_async_copy(mixed, mixed_out, done.at[0])]
    keep[0].start()
    devices = got.shape[0]
    rows, size, channels = pair.shape
    width = math.isqrt(spread.shape[0] * spread.shape[1] // channels)
    groups = spread.shape[0] // width
    blocks = right_rows.shape[0]
    seqs = blocks * LANES // size
    for slot, peer in enumerate(order):
        for block in range(blocks):
            right_rows[block, pl.ds(peer, width, stride=devices), :] = got[
                slot, block * width : (block + 1) * width, :
            ].astype(F32)
        left_rows[pl.ds(peer, seqs * rows, stride=devices), :] = got[slot, blocks * width :, :].astype(F32)
    right = jnp.concatenate([jnp.transpose(right_rows[block]) for block in range(blocks)], axis=0).astype(BF16)
    copies = LANES // width
    tiles = groups // copies
    lane = lax.broadcasted_iota(jnp.int32, (seqs * PAIR * devices, LANES), 1)
    blank = jnp.zeros((seqs * PAIR * devices, LANES), BF16)
    pieces = []
    for first in range(0, rows, PAIR):
        begins = [(s * rows + first + i) * devices for s in range(seqs) for i in range(PAIR)]
        left = jnp.concatenate([left_rows[begin : begin + devices, :] for begin in begins], axis=0)
        for group in range(groups):
            mine = jnp.where(lane // width == group % copies, left, 0.0).astype(BF16)
            pieces.append(jnp.concatenate([mine if n == group // copies else blank for n in range(tiles)], axis=1))
    table = dot(jnp.concatenate(pieces, axis=0), spread[...], NN)
    for first in range(0, rows, PAIR):
        update = jnp.zeros((size, PAIR * channels), F32)
        for s in range(seqs):
            columns = []
            for i in range(PAIR):
                column = []
                for e in range(width):
                    group, place = e // (width // groups), e % (width // groups)
                    begin = ((first // PAIR * groups + group) * seqs * PAIR + s * PAIR + i) * devices
                    column.append(table[begin : begin + devices, place * channels : (place + 1) * channels])
                columns.append(jnp.concatenate(column, axis=0).astype(BF16))
            columns = jnp.concatenate(columns, axis=1)
            update = update + dot(right[s * size : (s + 1) * size, :], columns, NN)
        for i in range(PAIR):
            here = update[:, i * channels : (i + 1) * channels]
            out[first + i] = (pair[first + i] + scale[first + i] * here).astype(BF16)
        ready = pl.ds(first, PAIR)
        keep.append(pltpu.make_async_copy(out.at[ready], out_far.at[ready], done.at[1 + first // PAIR]))
        keep[-1].start()
    for copy in keep:
        copy.wait()


def member_order(devices):
    return [(5 * devices // 8 - n) % devices for n in range(devices)]


def vmem(count):
    return [pl.BlockSpec(memory_space=pltpu.VMEM) for _ in range(count)]


def call(body, shapes, in_specs, name, flops, moved, scratch=(), limit=VMEM_LIMIT):
    return pl.pallas_call(
        body,
        out_shape=shapes,
        in_specs=in_specs,
        out_specs=jax.tree.map(lambda _: pl.BlockSpec(memory_space=pltpu.VMEM), shapes),
        scratch_shapes=list(scratch),
        compiler_params=pltpu.CompilerParams(vmem_limit_bytes=limit),
        cost_estimate=pl.CostEstimate(flops=flops, bytes_accessed=moved, transcendentals=0),
        name=name,
    )


def on_device(
    alignment_features,
    couple_features,
    alignment_presence,
    amino_presence,
    strand_identity,
    strand_couple_embedding,
    fourfold_input_matrix,
    heads_merge_matrix,
    couple_logit_matrix,
    twin_factor_matrix,
    tensor_reduce_matrix,
):
    rows, size, channels = couple_features.shape
    seqs, _, depth = alignment_features.shape
    devices = size // rows
    heads = couple_logit_matrix.shape[1]
    merged = heads_merge_matrix.shape[0]
    width = twin_factor_matrix.shape[1] // 2
    group = heads * rows
    pack = LANES // group
    struct = jax.ShapeDtypeStruct
    order = member_order(devices)
    ids_row = strand_identity.reshape(1, size)
    amino_row = amino_presence.reshape(1, size)

    arguments = (
        couple_features,
        couple_logit_matrix.T,
        ids_row,
        strand_couple_embedding,
        alignment_features,
        fourfold_input_matrix,
        alignment_presence,
        amino_row,
        tensor_reduce_matrix,
        heads_merge_matrix,
        twin_factor_matrix.T,
    )
    bias, couple, ids_row, emb, x, weights, presence, amino_row, reduce, merge, twin = call(
        bias_kernel,
        (struct((devices, size // pack, LANES), BF16),)
        + tuple(pltpu.VMEM(array.shape, array.dtype) for array in arguments[:1] + arguments[2:]),
        [pl.BlockSpec(memory_space=pltpu.HBM)] * len(arguments),
        "pair_bias",
        2 * rows * size * channels * LANES,
        2 * rows * size * channels,
        [
            pltpu.VMEM(arguments[1].shape, BF16),
            pltpu.VMEM((size, channels), F32),
            pltpu.SemaphoreType.DMA((len(arguments) + rows,)),
        ],
    )(*[pltpu.with_memory_space_constraint(array, pltpu.HBM) for array in arguments])
    bias = lax.all_to_all(bias, "dap", 0, 0, axis_index_groups=[order])

    blocks = seqs * size // LANES
    mixed, factors, pair, scale, spread = call(
        functools.partial(middle_kernel, order),
        (
            pltpu.VMEM(alignment_features.shape, BF16),
            struct((devices, blocks * width + seqs * rows, LANES), BF16),
            struct(couple_features.shape, F32),
            struct(couple_features.shape, F32),
            struct((GROUPS * width, width // GROUPS * channels), BF16),
        ),
        vmem(11),
        "attend",
        2 * seqs * size * depth * 4 * merged + 6 * seqs * size * size * heads * merged,
        2 * depth * 4 * merged + 8 * seqs * size * size * heads,
        [
            pltpu.VMEM((seqs, size, heads * size), F32),
            pltpu.VMEM((seqs, size, merged), BF16),
            pltpu.VMEM((seqs, size, merged), F32),
            pltpu.VMEM((seqs, size, LANES), F32),
            pltpu.VMEM((1, seqs * size), F32),
            pltpu.VMEM((width * width, channels), F32),
            pltpu.VMEM((size, channels), F32),
            pltpu.VMEM((size, channels), F32),
        ],
    )(bias, x, weights, presence, ids_row, amino_row, emb, couple, reduce, merge, twin)
    factors = lax.all_to_all(factors, "dap", 0, 0, axis_index_groups=[order])

    refreshed, mixed = pl.pallas_call(
        functools.partial(outer_kernel, order),
        out_shape=(struct(couple_features.shape, BF16), struct(alignment_features.shape, BF16)),
        in_specs=vmem(5),
        out_specs=(pl.BlockSpec(memory_space=pl.ANY), pl.BlockSpec(memory_space=pl.ANY)),
        scratch_shapes=[
            pltpu.VMEM((blocks, width * devices, LANES), F32),
            pltpu.VMEM((seqs * rows * devices, LANES), F32),
            pltpu.VMEM(couple_features.shape, BF16),
            pltpu.SemaphoreType.DMA((1 + rows // PAIR,)),
        ],
        compiler_params=pltpu.CompilerParams(vmem_limit_bytes=VMEM_LIMIT),
        cost_estimate=pl.CostEstimate(
            flops=4 * rows * size * channels * width * seqs * devices,
            bytes_accessed=16 * rows * size * channels,
            transcendentals=0,
        ),
        name="outer_mean",
    )(factors, spread, pair, scale, mixed)
    return (mixed, refreshed)


def solution(mesh):
    in_specs = (
        P(("cplx", "dap"), None, None),
        P(("cplx", "dap"), None, None),
        P("cplx", None),
        P("cplx"),
        P("cplx"),
        P(),
        P(),
        P(),
        P(),
        P(),
        P(),
    )
    out_specs = (P(("cplx", "dap"), None, None), P(("cplx", "dap"), None, None))
    return jax.shard_map(
        on_device, mesh=mesh, in_specs=in_specs, out_specs=out_specs, check_vma=False
    )
```

```python
import functools
import math

import jax
import jax.numpy as jnp
from jax import lax
from jax.experimental import pallas as pl
from jax.experimental.pallas import tpu as pltpu
from jax.sharding import PartitionSpec as P

EPS = 1e-05
LANES = 128
F32 = jnp.float32
BF16 = jnp.bfloat16
VMEM_LIMIT = 24 * 1024 * 1024
GROUPS = 8
PAIR = 2
VMEM_FULL = 63 * 1024 * 1024


def standardize(x):
    center = x - jnp.mean(x, axis=-1, keepdims=True)
    spread = jnp.mean(center * center, axis=-1, keepdims=True)
    return center * lax.rsqrt(spread + EPS)


def to_column(row, size):
    down = lax.broadcasted_iota(jnp.int32, (size, size), 0)
    across = lax.broadcasted_iota(jnp.int32, (size, size), 1)
    spread = jnp.where(down == across, jnp.broadcast_to(row, (size, size)), 0.0)
    return jnp.sum(spread, axis=1, keepdims=True)


def dot(a, b, contract):
    return lax.dot_general(a, b, (contract, ((), ())), preferred_element_type=F32)


NN = ((1,), (0,))
NT = ((1,), (1,))
TN = ((0,), (0,))


def pair_input(ids_row, emb, x, chains, res_start):
    rows, size, channels = x.shape
    chain = jnp.broadcast_to(to_column(ids_row[...].astype(F32), size), (size, channels))
    chains[...] = chain
    other, same = emb[0:1, :], emb[1:2, :]
    for i in range(rows):
        chain_i = chains[pl.ds(res_start + i, 1), :]
        yield x[i].astype(F32) + jnp.where(chain == chain_i, same, other)


def bias_kernel(*refs):
    count = (len(refs) - 3) // 2
    far, out, near = refs[:count], refs[count], refs[count + 1 : 2 * count]
    logit, chains, arrived = refs[-3:]
    x, ids_row, emb = near[:3]
    near = (x, logit, ids_row, emb) + near[3:]
    rows, size, _ = x.shape
    each = max(1, rows // 4)
    moves = [(far[0].at[pl.ds(b, each)], x.at[pl.ds(b, each)]) for b in range(0, rows, each)]
    first = len(moves) + 3
    moves += list(zip(far[1:], near[1:]))
    copies = [pltpu.make_async_copy(src, dst, arrived.at[n]) for n, (src, dst) in enumerate(moves)]
    for copy in copies:
        copy.start()
    for copy in copies[:first]:
        copy.wait()
    heads = logit.shape[0]
    group = heads * rows
    pack = LANES // group
    part = size // pack
    res_start = lax.axis_index("dap") * rows
    table = logit[...].astype(F32)
    wide = [jnp.broadcast_to(table[h : h + 1, :], (rows, table.shape[1])) for h in range(heads)] * pack
    wide = jnp.concatenate(wide, axis=0).astype(BF16)
    normed = [standardize(z).astype(BF16) for z in pair_input(ids_row, emb, x, chains, res_start)]
    full = dot(jnp.concatenate(normed, axis=0), wide, NT)
    lane = lax.broadcasted_iota(jnp.int32, (part, LANES), 1)
    total = jnp.zeros((part, LANES), F32)
    for i in range(rows):
        for half in range(pack):
            begin = i * size + half * part
            pick = (lane // group == half) & (lane % rows == i)
            total = jnp.where(pick, full[begin : begin + part, :], total)
    total = total.astype(BF16)
    for peer in range(out.shape[0]):
        out[peer] = total
    for copy in copies[first:]:
        copy.wait()


def prepare(ids_row, amino_row, emb, x, presence, reduce, pair, scale, spread, wide, chains, keeps):
    rows, size, channels = x.shape
    width = spread.shape[0] // GROUPS
    res_start = lax.axis_index("dap") * rows
    for i, z in enumerate(pair_input(ids_row, emb, x, chains, res_start)):
        pair[i] = z
    here = presence[...].astype(BF16)
    count = dot(here, here, TN)
    lane = lax.broadcasted_iota(jnp.int32, (size, size), 1)
    kept = jnp.broadcast_to(to_column(amino_row[...].astype(F32), size), (size, channels))
    keeps[...] = kept
    for i in range(rows):
        column = jnp.sum(jnp.where(lane == res_start + i, count, 0.0), axis=1, keepdims=True) + 1.0
        scale[i] = kept * keeps[pl.ds(res_start + i, 1), :] / column
    turned = jnp.swapaxes(reduce[...].reshape(width, width, channels), 0, 1)
    each = width // GROUPS
    for e in range(width):
        group, place = e // each, e % each
        spread[group * width : (group + 1) * width, place * channels : (place + 1) * channels] = turned[
            e
        ].astype(BF16)


def project(
    x,
    weights,
    presence,
    ids_row,
    amino_row,
    emb,
    couple,
    reduce,
    scores,
    content,
    gate,
    present,
    present_row,
    pair,
    scale,
    spread,
    wide,
    chains,
    keeps,
):
    seqs, size, depth = x.shape
    rows = couple.shape[0]
    merged = content.shape[2]
    group_total = scores.shape[2]
    heads = group_total // size
    head_size = merged // heads
    seq_start = lax.axis_index("dap") * seqs
    normed = standardize(x[...].reshape(seqs * size, depth).astype(F32)).astype(BF16)
    mapped = dot(normed, weights[...], NN)
    asking = (mapped[:, :merged] * head_size**-0.5).astype(BF16).astype(F32)
    target = mapped[:, merged : 2 * merged].astype(BF16)
    content[...] = mapped[:, 2 * merged : 3 * merged].astype(BF16).reshape(content.shape)
    gate[...] = jax.nn.sigmoid(mapped[:, 3 * merged :]).reshape(gate.shape)
    lane = lax.broadcasted_iota(jnp.int32, (rows, merged), 1)
    row_pieces = []
    for s in range(seqs):
        pieces = []
        for begin in range(s * size, (s + 1) * size, rows):
            here = asking[begin : begin + rows, :]
            for h in range(heads):
                pieces.append(jnp.where(lane // head_size == h, here, 0.0))
        masked = jnp.concatenate(pieces, axis=0).astype(BF16)
        scores[s] = dot(target[s * size : (s + 1) * size, :], masked, NT)
        row = presence[pl.ds(seq_start + s, 1), :].astype(F32)
        present[s] = jnp.broadcast_to(to_column(row, size), (size, LANES))
        row_pieces.append(row)
    present_row[...] = jnp.concatenate(row_pieces, axis=1)
    prepare(ids_row, amino_row, emb, couple, presence, reduce, pair, scale, spread, wide, chains, keeps)


def attend(order, bias, scores, content, gate, present, present_row, x, merge, twin, mixed, out):
    devices, part, _ = bias.shape
    seqs, size, depth = x.shape
    merged = content.shape[2]
    pack = size // part
    group = LANES // pack
    rows = size // devices
    heads = group // rows
    head_size = merged // heads
    width = twin.shape[0] // 2
    lane = lax.broadcasted_iota(jnp.int32, (rows, LANES), 1)
    gated = []
    tables = []
    for block in range(devices // pack):
        got = [bias[order.index(block * pack + n)].astype(F32) for n in range(pack)]
        tables.append(
            jnp.concatenate(
                [
                    jnp.concatenate([g[:, half * group : (half + 1) * group] for g in got], axis=1)
                    for half in range(pack)
                ],
                axis=0,
            )
        )
    tiles = merged // LANES
    few = heads // tiles
    for s in range(seqs):
        absent = (present[s] - 1.0) * 1000000000.0
        turned = []
        for block in range(devices // pack):
            logits = scores[s, :, block * LANES : (block + 1) * LANES] + tables[block] + absent
            raised = jnp.exp(logits - jnp.max(logits, axis=0, keepdims=True))
            weights = raised * (1.0 / jnp.sum(raised, axis=0, keepdims=True))
            turned.append(jnp.transpose(weights.astype(BF16)))
        context = []
        for tile in range(tiles):
            mine = []
            for block in range(devices // pack):
                for n in range(pack):
                    begin = n * group + tile * few * rows
                    mine.append(turned[block][begin : begin + few * rows, :])
            product = dot(jnp.concatenate(mine, axis=0), content[s, :, tile * LANES : (tile + 1) * LANES], NN)
            picked = []
            for peer in range(devices):
                total = product[peer * few * rows : peer * few * rows + rows, :]
                for h in range(1, few):
                    begin = (peer * few + h) * rows
                    total = jnp.where(lane // head_size == h, product[begin : begin + rows, :], total)
                picked.append(total)
            context.append(jnp.concatenate(picked, axis=0))
        gated.append((gate[s] * jnp.concatenate(context, axis=1)).astype(BF16))
    offset = dot(jnp.concatenate(gated, axis=0), merge[...], NN)
    updated = (x[...].reshape(seqs * size, depth).astype(F32) + offset).astype(BF16)
    mixed[...] = updated.reshape(mixed.shape)
    normed = standardize(updated.astype(F32)).astype(BF16)
    left = dot(normed, jnp.concatenate([twin[:width, :]] * (LANES // width), axis=0), NT)
    right = (dot(twin[width:, :], normed, NT) * present_row[...]).astype(BF16)
    blocks = seqs * size // LANES
    for peer in range(devices):
        for block in range(blocks):
            out[peer, block * width : (block + 1) * width, :] = right[:, block * LANES : (block + 1) * LANES]
    for slot, peer in enumerate(order):
        rows_here = []
        for s in range(seqs):
            begin = peer * rows
            here = left[s * size + begin : s * size + begin + rows, :]
            rows_here.append(here * present[s, begin : begin + rows, :])
        out[slot, blocks * width :, :] = jnp.concatenate(rows_here, axis=0).astype(BF16)


def middle_kernel(
    order,
    bias,
    x,
    weights,
    presence,
    ids_row,
    amino_row,
    emb,
    couple,
    reduce,
    merge,
    twin,
    mixed,
    out,
    pair,
    scale,
    spread,
    scores,
    content,
    gate,
    present,
    present_row,
    wide,
    chains,
    keeps,
):
    kept = (scores, content, gate, present, present_row)
    project(
        x, weights, presence, ids_row, amino_row, emb, couple, reduce, *kept, pair, scale, spread, wide, chains, keeps
    )
    attend(order, bias, *kept, x, merge, twin, mixed, out)


def outer_kernel(order, got, spread, pair, scale, mixed, out_far, mixed_out, right_rows, left_rows, out, done):
    keep = [pltpu.make_async_copy(mixed, mixed_out, done.at[0])]
    keep[0].start()
    devices = got.shape[0]
    rows, size, channels = pair.shape
    width = math.isqrt(spread.shape[0] * spread.shape[1] // channels)
    groups = spread.shape[0] // width
    blocks = right_rows.shape[0]
    seqs = blocks * LANES // size
    for slot, peer in enumerate(order):
        for block in range(blocks):
            right_rows[block, pl.ds(peer, width, stride=devices), :] = got[
                slot, block * width : (block + 1) * width, :
            ].astype(F32)
        left_rows[pl.ds(peer, seqs * rows, stride=devices), :] = got[slot, blocks * width :, :].astype(F32)
    right = jnp.concatenate([jnp.transpose(right_rows[block]) for block in range(blocks)], axis=0).astype(BF16)
    copies = LANES // width
    tiles = groups // copies
    lane = lax.broadcasted_iota(jnp.int32, (seqs * PAIR * devices, LANES), 1)
    blank = jnp.zeros((seqs * PAIR * devices, LANES), BF16)
    pieces = []
    for first in range(0, rows, PAIR):
        begins = [(s * rows + first + i) * devices for s in range(seqs) for i in range(PAIR)]
        left = jnp.concatenate([left_rows[begin : begin + devices, :] for begin in begins], axis=0)
        for group in range(groups):
            mine = jnp.where(lane // width == group % copies, left, 0.0).astype(BF16)
            pieces.append(jnp.concatenate([mine if n == group // copies else blank for n in range(tiles)], axis=1))
    table = dot(jnp.concatenate(pieces, axis=0), spread[...], NN)
    for first in range(0, rows, PAIR):
        update = jnp.zeros((size, PAIR * channels), F32)
        for s in range(seqs):
            columns = []
            for i in range(PAIR):
                column = []
                for e in range(width):
                    group, place = e // (width // groups), e % (width // groups)
                    begin = ((first // PAIR * groups + group) * seqs * PAIR + s * PAIR + i) * devices
                    column.append(table[begin : begin + devices, place * channels : (place + 1) * channels])
                columns.append(jnp.concatenate(column, axis=0).astype(BF16))
            columns = jnp.concatenate(columns, axis=1)
            update = update + dot(right[s * size : (s + 1) * size, :], columns, NN)
        for i in range(PAIR):
            here = update[:, i * channels : (i + 1) * channels]
            out[first + i] = (pair[first + i] + scale[first + i] * here).astype(BF16)
        ready = pl.ds(first, PAIR)
        keep.append(pltpu.make_async_copy(out.at[ready], out_far.at[ready], done.at[1 + first // PAIR]))
        keep[-1].start()
    for copy in keep:
        copy.wait()


def member_order(devices):
    return [(5 * devices // 8 - n) % devices for n in range(devices)]


def vmem(count):
    return [pl.BlockSpec(memory_space=pltpu.VMEM) for _ in range(count)]


def call(body, shapes, in_specs, name, flops, moved, scratch=(), limit=VMEM_LIMIT):
    return pl.pallas_call(
        body,
        out_shape=shapes,
        in_specs=in_specs,
        out_specs=jax.tree.map(lambda _: pl.BlockSpec(memory_space=pltpu.VMEM), shapes),
        scratch_shapes=list(scratch),
        compiler_params=pltpu.CompilerParams(vmem_limit_bytes=limit),
        cost_estimate=pl.CostEstimate(flops=flops, bytes_accessed=moved, transcendentals=0),
        name=name,
    )


def on_device(
    alignment_features,
    couple_features,
    alignment_presence,
    amino_presence,
    strand_identity,
    strand_couple_embedding,
    fourfold_input_matrix,
    heads_merge_matrix,
    couple_logit_matrix,
    twin_factor_matrix,
    tensor_reduce_matrix,
):
    rows, size, channels = couple_features.shape
    seqs, _, depth = alignment_features.shape
    devices = size // rows
    heads = couple_logit_matrix.shape[1]
    merged = heads_merge_matrix.shape[0]
    width = twin_factor_matrix.shape[1] // 2
    group = heads * rows
    pack = LANES // group
    struct = jax.ShapeDtypeStruct
    order = member_order(devices)
    ids_row = strand_identity.reshape(1, size)
    amino_row = amino_presence.reshape(1, size)

    arguments = (
        couple_features,
        couple_logit_matrix.T,
        ids_row,
        strand_couple_embedding,
        alignment_features,
        fourfold_input_matrix,
        alignment_presence,
        amino_row,
        tensor_reduce_matrix,
        heads_merge_matrix,
        twin_factor_matrix.T,
    )
    bias, couple, ids_row, emb, x, weights, presence, amino_row, reduce, merge, twin = call(
        bias_kernel,
        (struct((devices, size // pack, LANES), BF16),)
        + tuple(pltpu.VMEM(array.shape, array.dtype) for array in arguments[:1] + arguments[2:]),
        [pl.BlockSpec(memory_space=pltpu.HBM)] * len(arguments),
        "pair_bias",
        2 * rows * size * channels * LANES,
        2 * rows * size * channels,
        [
            pltpu.VMEM(arguments[1].shape, BF16),
            pltpu.VMEM((size, channels), F32),
            pltpu.SemaphoreType.DMA((len(arguments) + rows,)),
        ],
    )(*[pltpu.with_memory_space_constraint(array, pltpu.HBM) for array in arguments])
    bias = lax.all_to_all(bias, "dap", 0, 0, axis_index_groups=[order])

    blocks = seqs * size // LANES
    mixed, factors, pair, scale, spread = call(
        functools.partial(middle_kernel, order),
        (
            pltpu.VMEM(alignment_features.shape, BF16),
            struct((devices, blocks * width + seqs * rows, LANES), BF16),
            struct(couple_features.shape, F32),
            struct(couple_features.shape, F32),
            struct((GROUPS * width, width // GROUPS * channels), BF16),
        ),
        vmem(11),
        "attend",
        2 * seqs * size * depth * 4 * merged + 6 * seqs * size * size * heads * merged,
        2 * depth * 4 * merged + 8 * seqs * size * size * heads,
        [
            pltpu.VMEM((seqs, size, heads * size), F32),
            pltpu.VMEM((seqs, size, merged), BF16),
            pltpu.VMEM((seqs, size, merged), F32),
            pltpu.VMEM((seqs, size, LANES), F32),
            pltpu.VMEM((1, seqs * size), F32),
            pltpu.VMEM((width * width, channels), F32),
            pltpu.VMEM((size, channels), F32),
            pltpu.VMEM((size, channels), F32),
        ],
    )(bias, x, weights, presence, ids_row, amino_row, emb, couple, reduce, merge, twin)
    factors = lax.all_to_all(factors, "dap", 0, 0, axis_index_groups=[order])

    refreshed, mixed = pl.pallas_call(
        functools.partial(outer_kernel, order),
        out_shape=(struct(couple_features.shape, BF16), struct(alignment_features.shape, BF16)),
        in_specs=vmem(5),
        out_specs=(pl.BlockSpec(memory_space=pl.ANY), pl.BlockSpec(memory_space=pl.ANY)),
        scratch_shapes=[
            pltpu.VMEM((blocks, width * devices, LANES), F32),
            pltpu.VMEM((seqs * rows * devices, LANES), F32),
            pltpu.VMEM(couple_features.shape, BF16),
            pltpu.SemaphoreType.DMA((1 + rows // PAIR,)),
        ],
        compiler_params=pltpu.CompilerParams(vmem_limit_bytes=VMEM_LIMIT),
        cost_estimate=pl.CostEstimate(
            flops=4 * rows * size * channels * width * seqs * devices,
            bytes_accessed=16 * rows * size * channels,
            transcendentals=0,
        ),
        name="outer_mean",
    )(factors, spread, pair, scale, mixed)
    return (mixed, refreshed)


def solution(mesh):
    in_specs = (
        P(("cplx", "dap"), None, None),
        P(("cplx", "dap"), None, None),
        P("cplx", None),
        P("cplx"),
        P("cplx"),
        P(),
        P(),
        P(),
        P(),
        P(),
        P(),
    )
    out_specs = (P(("cplx", "dap"), None, None), P(("cplx", "dap"), None, None))
    return jax.shard_map(
        on_device, mesh=mesh, in_specs=in_specs, out_specs=out_specs, check_vma=False
    )
```

```python
import functools
import math

import jax
import jax.numpy as jnp
from jax import lax
from jax.experimental import pallas as pl
from jax.experimental.pallas import tpu as pltpu
from jax.sharding import PartitionSpec as P

EPS = 1e-05
LANES = 128
F32 = jnp.float32
BF16 = jnp.bfloat16
VMEM_LIMIT = 24 * 1024 * 1024
GROUPS = 8
PAIR = 2
VMEM_FULL = 63 * 1024 * 1024


def standardize(x):
    center = x - jnp.mean(x, axis=-1, keepdims=True)
    spread = jnp.mean(center * center, axis=-1, keepdims=True)
    return center * lax.rsqrt(spread + EPS)


def to_column(row, size):
    down = lax.broadcasted_iota(jnp.int32, (size, size), 0)
    across = lax.broadcasted_iota(jnp.int32, (size, size), 1)
    spread = jnp.where(down == across, jnp.broadcast_to(row, (size, size)), 0.0)
    return jnp.sum(spread, axis=1, keepdims=True)


def dot(a, b, contract):
    return lax.dot_general(a, b, (contract, ((), ())), preferred_element_type=F32)


NN = ((1,), (0,))
NT = ((1,), (1,))
TN = ((0,), (0,))


def pair_input(ids_row, emb, x, chains, res_start):
    rows, size, channels = x.shape
    chain = jnp.broadcast_to(to_column(ids_row[...].astype(F32), size), (size, channels))
    chains[...] = chain
    other, same = emb[0:1, :], emb[1:2, :]
    for i in range(rows):
        chain_i = chains[pl.ds(res_start + i, 1), :]
        yield x[i].astype(F32) + jnp.where(chain == chain_i, same, other)


def bias_kernel(*refs):
    count = (len(refs) - 3) // 2
    far, out, near = refs[:count], refs[count], refs[count + 1 : 2 * count]
    logit, chains, arrived = refs[-3:]
    x, ids_row, emb = near[:3]
    near = (x, logit, ids_row, emb) + near[3:]
    rows, size, _ = x.shape
    each = max(1, rows // 4)
    moves = [(far[0].at[pl.ds(b, each)], x.at[pl.ds(b, each)]) for b in range(0, rows, each)]
    first = len(moves) + 3
    moves += list(zip(far[1:], near[1:]))
    copies = [pltpu.make_async_copy(src, dst, arrived.at[n]) for n, (src, dst) in enumerate(moves)]
    for copy in copies:
        copy.start()
    for copy in copies[:first]:
        copy.wait()
    heads = logit.shape[0]
    group = heads * rows
    pack = LANES // group
    part = size // pack
    res_start = lax.axis_index("dap") * rows
    table = logit[...].astype(F32)
    wide = [jnp.broadcast_to(table[h : h + 1, :], (rows, table.shape[1])) for h in range(heads)] * pack
    wide = jnp.concatenate(wide, axis=0).astype(BF16)
    normed = [standardize(z).astype(BF16) for z in pair_input(ids_row, emb, x, chains, res_start)]
    full = dot(jnp.concatenate(normed, axis=0), wide, NT)
    lane = lax.broadcasted_iota(jnp.int32, (part, LANES), 1)
    total = jnp.zeros((part, LANES), F32)
    for i in range(rows):
        for half in range(pack):
            begin = i * size + half * part
            pick = (lane // group == half) & (lane % rows == i)
            total = jnp.where(pick, full[begin : begin + part, :], total)
    total = total.astype(BF16)
    for peer in range(out.shape[0]):
        out[peer] = total
    for copy in copies[first:]:
        copy.wait()


def prepare(ids_row, amino_row, emb, x, presence, reduce, pair, scale, spread, chains):
    rows, size, channels = x.shape
    width = spread.shape[0] // GROUPS
    res_start = lax.axis_index("dap") * rows
    for i, z in enumerate(pair_input(ids_row, emb, x, chains, res_start)):
        pair[i] = z
    here = presence[...].astype(BF16)
    count = dot(here, here, TN)
    lane = lax.broadcasted_iota(jnp.int32, (size, size), 1)
    kept = amino_row[...].astype(F32)
    ratio = to_column(kept, size) * kept / (count + 1.0)
    for i in range(rows):
        column = jnp.sum(jnp.where(lane == res_start + i, ratio, 0.0), axis=1, keepdims=True)
        scale[i] = jnp.broadcast_to(column, (size, channels))
    turned = jnp.swapaxes(reduce[...].reshape(width, width, channels), 0, 1)
    each = width // GROUPS
    for e in range(width):
        group, place = e // each, e % each
        spread[group * width : (group + 1) * width, place * channels : (place + 1) * channels] = turned[
            e
        ].astype(BF16)


def project(
    x,
    weights,
    presence,
    ids_row,
    amino_row,
    emb,
    couple,
    reduce,
    scores,
    content,
    gate,
    present,
    present_row,
    pair,
    scale,
    spread,
    chains,
):
    seqs, size, depth = x.shape
    rows = couple.shape[0]
    merged = content.shape[2]
    group_total = scores.shape[2]
    heads = group_total // size
    head_size = merged // heads
    seq_start = lax.axis_index("dap") * seqs
    normed = standardize(x[...].reshape(seqs * size, depth).astype(F32)).astype(BF16)
    mapped = dot(normed, weights[...], NN)
    asking = (mapped[:, :merged] * head_size**-0.5).astype(BF16).astype(F32)
    target = mapped[:, merged : 2 * merged].astype(BF16)
    content[...] = mapped[:, 2 * merged : 3 * merged].astype(BF16).reshape(content.shape)
    gate[...] = jax.nn.sigmoid(mapped[:, 3 * merged :]).reshape(gate.shape)
    lane = lax.broadcasted_iota(jnp.int32, (rows, merged), 1)
    row_pieces = []
    for s in range(seqs):
        pieces = []
        for begin in range(s * size, (s + 1) * size, rows):
            here = asking[begin : begin + rows, :]
            for h in range(heads):
                pieces.append(jnp.where(lane // head_size == h, here, 0.0))
        masked = jnp.concatenate(pieces, axis=0).astype(BF16)
        scores[s] = dot(target[s * size : (s + 1) * size, :], masked, NT)
        row = presence[pl.ds(seq_start + s, 1), :].astype(F32)
        present[s] = jnp.broadcast_to(to_column(row, size), (size, LANES))
        row_pieces.append(row)
    present_row[...] = jnp.concatenate(row_pieces, axis=1)
    prepare(ids_row, amino_row, emb, couple, presence, reduce, pair, scale, spread, chains)


def attend(order, bias, scores, content, gate, present, present_row, x, merge, twin, mixed, out):
    devices, part, _ = bias.shape
    seqs, size, depth = x.shape
    merged = content.shape[2]
    pack = size // part
    group = LANES // pack
    rows = size // devices
    heads = group // rows
    head_size = merged // heads
    width = twin.shape[0] // 2
    lane = lax.broadcasted_iota(jnp.int32, (rows, LANES), 1)
    gated = []
    tables = []
    for block in range(devices // pack):
        got = [bias[order.index(block * pack + n)].astype(F32) for n in range(pack)]
        tables.append(
            jnp.concatenate(
                [
                    jnp.concatenate([g[:, half * group : (half + 1) * group] for g in got], axis=1)
                    for half in range(pack)
                ],
                axis=0,
            )
        )
    tiles = merged // LANES
    few = heads // tiles
    for s in range(seqs):
        absent = (present[s] - 1.0) * 1000000000.0
        turned = []
        for block in range(devices // pack):
            logits = scores[s, :, block * LANES : (block + 1) * LANES] + tables[block] + absent
            raised = jnp.exp(logits - jnp.max(logits, axis=0, keepdims=True))
            weights = raised * (1.0 / jnp.sum(raised, axis=0, keepdims=True))
            turned.append(jnp.transpose(weights.astype(BF16)))
        context = []
        for tile in range(tiles):
            mine = []
            for block in range(devices // pack):
                for n in range(pack):
                    begin = n * group + tile * few * rows
                    mine.append(turned[block][begin : begin + few * rows, :])
            product = dot(jnp.concatenate(mine, axis=0), content[s, :, tile * LANES : (tile + 1) * LANES], NN)
            picked = []
            for peer in range(devices):
                total = product[peer * few * rows : peer * few * rows + rows, :]
                for h in range(1, few):
                    begin = (peer * few + h) * rows
                    total = jnp.where(lane // head_size == h, product[begin : begin + rows, :], total)
                picked.append(total)
            context.append(jnp.concatenate(picked, axis=0))
        gated.append((gate[s] * jnp.concatenate(context, axis=1)).astype(BF16))
    offset = dot(jnp.concatenate(gated, axis=0), merge[...], NN)
    updated = (x[...].reshape(seqs * size, depth).astype(F32) + offset).astype(BF16)
    mixed[...] = updated.reshape(mixed.shape)
    normed = standardize(updated.astype(F32)).astype(BF16)
    left = dot(normed, jnp.concatenate([twin[:width, :]] * (LANES // width), axis=0), NT)
    right = (dot(twin[width:, :], normed, NT) * present_row[...]).astype(BF16)
    blocks = seqs * size // LANES
    for peer in range(devices):
        for block in range(blocks):
            out[peer, block * width : (block + 1) * width, :] = right[:, block * LANES : (block + 1) * LANES]
    for slot, peer in enumerate(order):
        rows_here = []
        for s in range(seqs):
            begin = peer * rows
            here = left[s * size + begin : s * size + begin + rows, :]
            rows_here.append(here * present[s, begin : begin + rows, :])
        out[slot, blocks * width :, :] = jnp.concatenate(rows_here, axis=0).astype(BF16)


def middle_kernel(
    order,
    bias,
    x,
    weights,
    presence,
    ids_row,
    amino_row,
    emb,
    couple,
    reduce,
    merge,
    twin,
    mixed,
    out,
    pair,
    scale,
    spread,
    scores,
    content,
    gate,
    present,
    present_row,
    chains,
):
    kept = (scores, content, gate, present, present_row)
    project(
        x, weights, presence, ids_row, amino_row, emb, couple, reduce, *kept, pair, scale, spread, chains
    )
    attend(order, bias, *kept, x, merge, twin, mixed, out)


def outer_kernel(order, got, spread, pair, scale, mixed, out_far, mixed_out, right_rows, left_rows, out, done):
    keep = [pltpu.make_async_copy(mixed, mixed_out, done.at[0])]
    keep[0].start()
    devices = got.shape[0]
    rows, size, channels = pair.shape
    width = math.isqrt(spread.shape[0] * spread.shape[1] // channels)
    groups = spread.shape[0] // width
    blocks = right_rows.shape[0]
    seqs = blocks * LANES // size
    inverse = [order.index(peer) for peer in range(devices)]
    for block in range(blocks):
        mine = jnp.stack([got[slot, block * width : (block + 1) * width, :].astype(F32) for slot in inverse])
        right_rows[block] = jnp.swapaxes(mine, 0, 1).reshape(width * devices, LANES)
    mine = jnp.stack([got[slot, blocks * width :, :].astype(F32) for slot in inverse])
    left_rows[...] = jnp.swapaxes(mine, 0, 1).reshape(left_rows.shape)
    right = jnp.concatenate([jnp.transpose(right_rows[block]) for block in range(blocks)], axis=0).astype(BF16)
    copies = LANES // width
    tiles = groups // copies
    lane = lax.broadcasted_iota(jnp.int32, (seqs * PAIR * devices, LANES), 1)
    blank = jnp.zeros((seqs * PAIR * devices, LANES), BF16)
    pieces = []
    for first in range(0, rows, PAIR):
        begins = [(s * rows + first + i) * devices for s in range(seqs) for i in range(PAIR)]
        left = jnp.concatenate([left_rows[begin : begin + devices, :] for begin in begins], axis=0)
        for group in range(groups):
            mine = jnp.where(lane // width == group % copies, left, 0.0).astype(BF16)
            pieces.append(jnp.concatenate([mine if n == group // copies else blank for n in range(tiles)], axis=1))
    table = dot(jnp.concatenate(pieces, axis=0), spread[...], NN)
    for first in range(0, rows, PAIR):
        update = jnp.zeros((size, PAIR * channels), F32)
        for s in range(seqs):
            columns = []
            for i in range(PAIR):
                column = []
                for e in range(width):
                    group, place = e // (width // groups), e % (width // groups)
                    begin = ((first // PAIR * groups + group) * seqs * PAIR + s * PAIR + i) * devices
                    column.append(table[begin : begin + devices, place * channels : (place + 1) * channels])
                columns.append(jnp.concatenate(column, axis=0).astype(BF16))
            columns = jnp.concatenate(columns, axis=1)
            update = update + dot(right[s * size : (s + 1) * size, :], columns, NN)
        for i in range(PAIR):
            here = update[:, i * channels : (i + 1) * channels]
            out[first + i] = (pair[first + i] + scale[first + i] * here).astype(BF16)
        ready = pl.ds(first, PAIR)
        keep.append(pltpu.make_async_copy(out.at[ready], out_far.at[ready], done.at[1 + first // PAIR]))
        keep[-1].start()
    for copy in keep:
        copy.wait()


def member_order(devices):
    return [(5 * devices // 8 - n) % devices for n in range(devices)]


def vmem(count):
    return [pl.BlockSpec(memory_space=pltpu.VMEM) for _ in range(count)]


def call(body, shapes, in_specs, name, flops, moved, scratch=(), limit=VMEM_LIMIT):
    return pl.pallas_call(
        body,
        out_shape=shapes,
        in_specs=in_specs,
        out_specs=jax.tree.map(lambda _: pl.BlockSpec(memory_space=pltpu.VMEM), shapes),
        scratch_shapes=list(scratch),
        compiler_params=pltpu.CompilerParams(vmem_limit_bytes=limit),
        cost_estimate=pl.CostEstimate(flops=flops, bytes_accessed=moved, transcendentals=0),
        name=name,
    )


def on_device(
    alignment_features,
    couple_features,
    alignment_presence,
    amino_presence,
    strand_identity,
    strand_couple_embedding,
    fourfold_input_matrix,
    heads_merge_matrix,
    couple_logit_matrix,
    twin_factor_matrix,
    tensor_reduce_matrix,
):
    rows, size, channels = couple_features.shape
    seqs, _, depth = alignment_features.shape
    devices = size // rows
    heads = couple_logit_matrix.shape[1]
    merged = heads_merge_matrix.shape[0]
    width = twin_factor_matrix.shape[1] // 2
    group = heads * rows
    pack = LANES // group
    struct = jax.ShapeDtypeStruct
    order = member_order(devices)
    ids_row = strand_identity.reshape(1, size)
    amino_row = amino_presence.reshape(1, size)

    arguments = (
        couple_features,
        couple_logit_matrix.T,
        ids_row,
        strand_couple_embedding,
        alignment_features,
        fourfold_input_matrix,
        alignment_presence,
        amino_row,
        tensor_reduce_matrix,
        heads_merge_matrix,
        twin_factor_matrix.T,
    )
    bias, couple, ids_row, emb, x, weights, presence, amino_row, reduce, merge, twin = call(
        bias_kernel,
        (struct((devices, size // pack, LANES), BF16),)
        + tuple(pltpu.VMEM(array.shape, array.dtype) for array in arguments[:1] + arguments[2:]),
        [pl.BlockSpec(memory_space=pltpu.HBM)] * len(arguments),
        "pair_bias",
        2 * rows * size * channels * LANES,
        2 * rows * size * channels,
        [
            pltpu.VMEM(arguments[1].shape, BF16),
            pltpu.VMEM((size, channels), F32),
            pltpu.SemaphoreType.DMA((len(arguments) + rows,)),
        ],
    )(*[pltpu.with_memory_space_constraint(array, pltpu.HBM) for array in arguments])
    bias = lax.all_to_all(bias, "dap", 0, 0, axis_index_groups=[order])

    blocks = seqs * size // LANES
    mixed, factors, pair, scale, spread = call(
        functools.partial(middle_kernel, order),
        (
            pltpu.VMEM(alignment_features.shape, BF16),
            struct((devices, blocks * width + seqs * rows, LANES), BF16),
            struct(couple_features.shape, F32),
            struct(couple_features.shape, F32),
            struct((GROUPS * width, width // GROUPS * channels), BF16),
        ),
        vmem(11),
        "attend",
        2 * seqs * size * depth * 4 * merged + 6 * seqs * size * size * heads * merged,
        2 * depth * 4 * merged + 8 * seqs * size * size * heads,
        [
            pltpu.VMEM((seqs, size, heads * size), F32),
            pltpu.VMEM((seqs, size, merged), BF16),
            pltpu.VMEM((seqs, size, merged), F32),
            pltpu.VMEM((seqs, size, LANES), F32),
            pltpu.VMEM((1, seqs * size), F32),
            pltpu.VMEM((size, channels), F32),
        ],
    )(bias, x, weights, presence, ids_row, amino_row, emb, couple, reduce, merge, twin)
    factors = lax.all_to_all(factors, "dap", 0, 0, axis_index_groups=[order])

    refreshed, mixed = pl.pallas_call(
        functools.partial(outer_kernel, order),
        out_shape=(struct(couple_features.shape, BF16), struct(alignment_features.shape, BF16)),
        in_specs=vmem(5),
        out_specs=(pl.BlockSpec(memory_space=pl.ANY), pl.BlockSpec(memory_space=pl.ANY)),
        scratch_shapes=[
            pltpu.VMEM((blocks, width * devices, LANES), F32),
            pltpu.VMEM((seqs * rows * devices, LANES), F32),
            pltpu.VMEM(couple_features.shape, BF16),
            pltpu.SemaphoreType.DMA((1 + rows // PAIR,)),
        ],
        compiler_params=pltpu.CompilerParams(vmem_limit_bytes=VMEM_LIMIT),
        cost_estimate=pl.CostEstimate(
            flops=4 * rows * size * channels * width * seqs * devices,
            bytes_accessed=16 * rows * size * channels,
            transcendentals=0,
        ),
        name="outer_mean",
    )(factors, spread, pair, scale, mixed)
    return (mixed, refreshed)


def solution(mesh):
    in_specs = (
        P(("cplx", "dap"), None, None),
        P(("cplx", "dap"), None, None),
        P("cplx", None),
        P("cplx"),
        P("cplx"),
        P(),
        P(),
        P(),
        P(),
        P(),
        P(),
    )
    out_specs = (P(("cplx", "dap"), None, None), P(("cplx", "dap"), None, None))
    return jax.shard_map(
        on_device, mesh=mesh, in_specs=in_specs, out_specs=out_specs, check_vma=False
    )
```
